32 devices in a mesh: frame: 4 (over y, core), slab: 8 (over z, x).
Axes of the slice: x: 2, y: 2, z: 4, core: 2. Of those that a mesh axis runs over, the one named last changes fastest.
Arguments:
- element_data: bfloat16 [1024, 4, 512], P('slab', 'frame'), may hold values from -6 to 6
- migration: bfloat16 [2048, 1024], replicated, may hold values from -0.1875 to 0.1875
- column_gain: float32 [2048], replicated, may hold values from 0.3 to 3
- depth_gain: float32 [512], P('slab'), may hold values from 0.3 to 3
- coarse_shift: int32 [3, 4, 4, 8, 32], P(None, 'frame', None, None, 'slab'), may hold values from -8 to 8
- reference_frame: int32 [4], replicated, may hold values from 0 to 3, each once
Outputs:
- scores: float32 [7, 4, 4, 8, 32], P(None, 'frame', None, None, 'slab')
- displacement: float32 [3, 4, 4, 8, 32], P(None, 'frame', None, None, 'slab')
The draws below stay inside these ranges and needn't reach their ends.
Inputs may be any that keep to these rules, and one draw needn't show every extreme that they name: `reference_frame`: each frame index appears exactly once; the first entry names the reference frame, which serves all blocks.
All inputs are finite; a program needn't handle non-finite values.
Results may differ from the reference program's by a relative error of at most 0.0039.
Values may be sent and summed in bfloat16 or wider, within the bound.
No kernel may reach another device: no remote copies, remote signals or barrier semaphores. Data moves between devices by JAX's collectives and lax.ppermute only.
A program may use at most 64 MiB of HBM per device.

```python
import math
import jax
import jax.numpy as jnp
from jax import lax

ELEM = 1024
LX = 32
LY = 64
KX = 8
KY = 8
KZ = 16
CMAX = 8
FRAMES = 4
DEPTH = 512
BX = 4
BY = 8
BZ = 32


def place_ends(drawn, key, least, high):
    longest = drawn.shape.index(max(drawn.shape))
    spots = []
    for shift in (0, 1):
        where = [jax.random.randint(jax.random.fold_in(key, axis), (), 0, length) for axis, length in enumerate(drawn.shape)]
        where[longest] = (where[longest] + shift) % drawn.shape[longest]
        spots.append(tuple(where))
    return drawn.at[spots[0]].set(least).at[spots[1]].set(high)


def steps_of(own_key, dims, split, smallest, largest):
    def one(position, parts):
        draws = jax.random.uniform(jax.random.fold_in(jax.random.fold_in(own_key, 6), position), (parts,), jnp.float32, smallest / len(split), largest / len(split))
        return jnp.repeat(jnp.exp(draws), dims[position] // parts).reshape((-1,) + (1,) * (len(dims) - position - 1))

    level = one(*split[0])
    for cut in split[1:]:
        level = level * one(*cut)
    return level


def scatter_about(stream_key, shape, scale, limit, shards=(), kind=jnp.bfloat16):
    entries = scale * jax.random.normal(stream_key, shape, jnp.float32)
    if shards:
        entries = entries * steps_of(stream_key, shape, shards, -0.22, 0.18)
    return jnp.clip(entries, -limit, limit).astype(kind)


def setup_inputs(seed: int = 0) -> dict:
    key_of = jax.random.split(jax.random.key(seed), 7)
    return {
        "element_data": scatter_about(key_of[0], (ELEM, FRAMES, DEPTH), 1.0, 6.0, ((0, 8), (1, 4))),
        "migration": scatter_about(key_of[1], (LX * LY, ELEM), ELEM ** -0.5, 0.1875),
        "column_gain": jnp.clip(jnp.exp(jax.random.uniform(key_of[2], (LX * LY,), jnp.float32, math.log(0.3), math.log(3.0))), 0.3, 3.0),
        "depth_gain": jnp.clip(jnp.exp(math.log(3.0) - 2.3025851 * jax.random.uniform(key_of[3], (DEPTH,), jnp.float32) ** steps_of(key_of[3], (DEPTH,), ((0, 8),), -0.2, 0.2)), 0.3, 3.0),
        "coarse_shift": place_ends(jax.random.randint(key_of[4], (3, FRAMES, BX, BY, BZ), -CMAX, CMAX + 1), jax.random.fold_in(key_of[4], 1), -CMAX, CMAX).astype(jnp.int32),
        "reference_frame": jax.random.permutation(key_of[5], FRAMES).astype(jnp.int32),
    }


epsilon = 1e-05
shift_table = ((0, 0, 0), (-1, 0, 0), (1, 0, 0), (0, -1, 0), (0, 1, 0), (0, 0, -1), (0, 0, 1))

def block_scores(kernels, padded, starts):
    kernel_shape = kernels.shape[1:]
    box_shape = (kernel_shape[0] + 2, kernel_shape[1] + 2, kernel_shape[2] + 2)

    def take_box(first, second, third):
        return lax.dynamic_slice(padded, (first - 1, second - 1, third - 1), box_shape)
    boxes = jax.vmap(take_box)(starts[0], starts[1], starts[2])
    cell_count = kernel_shape[0] * kernel_shape[1] * kernel_shape[2]
    kernel_float = kernels.astype(jnp.float32)
    kernel_power = lax.optimization_barrier(jnp.mean(kernel_float * kernel_float, axis=(1, 2, 3)))
    results = []
    for shift_step in shift_table:
        low = [1 + shift_step[dimension] for dimension in range(3)]
        window = boxes[:, low[0]:low[0] + kernel_shape[0], low[1]:low[1] + kernel_shape[1], low[2]:low[2] + kernel_shape[2]].astype(jnp.float32)
        cross_mean = lax.optimization_barrier(jnp.mean(kernel_float * window, axis=(1, 2, 3)))
        window_power = lax.optimization_barrier(jnp.mean(window * window, axis=(1, 2, 3)))
        results.append(math.sqrt(cell_count) * cross_mean / jnp.sqrt((kernel_power + epsilon) * (window_power + epsilon)))
    return jnp.stack(results)

def refine(scores, shifts):
    refined = []
    for dimension in range(3):
        lower_score = scores[1 + 2 * dimension]
        upper_score = scores[2 + 2 * dimension]
        curvature = jnp.maximum(2.0 * scores[0] - lower_score - upper_score, 1.0)
        refined.append(shifts[dimension].astype(jnp.float32) + (upper_score - lower_score) / (2.0 * curvature))
    return jnp.stack(refined)

def reference(element_data, migration, column_gain, depth_gain, coarse_shift, reference_frame):

    def imaging(frame_number):
        samples = lax.dynamic_index_in_dim(element_data, frame_number, 1, keepdims=False)
        raw_image = jnp.dot(migration, samples, preferred_element_type=jnp.float32)
        return (raw_image * column_gain[:, None] * depth_gain[None, :]).astype(jnp.bfloat16)
    margin = CMAX + 1
    volume = imaging(reference_frame[0]).reshape(LX, LY, DEPTH)
    padded = jnp.pad(volume, margin)
    kernel_shape = (KX, KY, KZ)
    block_shape = (BX, BY, BZ)
    block_index = [lax.broadcasted_iota(jnp.int32, block_shape, dimension).reshape(-1) for dimension in range(3)]

    def per_frame(frame_number):
        image = imaging(frame_number)
        arranged = image.reshape(BX, KX, BY, KY, BZ, KZ).transpose(0, 2, 4, 1, 3, 5).reshape(-1, KX, KY, KZ)
        shifts = lax.dynamic_index_in_dim(coarse_shift, frame_number, 1, keepdims=False).reshape(3, -1)
        starts = [(block_index[dimension] * kernel_shape[dimension] + shifts[dimension] + margin).astype(jnp.int32) for dimension in range(3)]
        scores = block_scores(arranged, padded, starts)
        return (scores, refine(scores, shifts))
    scores, displacement = lax.map(per_frame, jnp.arange(FRAMES, dtype=jnp.int32))
    scores = scores.transpose(1, 0, 2).reshape(7, FRAMES, BX, BY, BZ)
    displacement = displacement.transpose(1, 0, 2).reshape(3, FRAMES, BX, BY, BZ)
    return (scores, displacement)
```

```python
import functools
import math

import jax
import jax.numpy as jnp
from jax import lax
from jax.experimental import pallas as pl
from jax.experimental.pallas import tpu as pltpu
from jax.sharding import PartitionSpec as P

LX = 32
LY = 64
KX = 8
KY = 8
KZ = 16
CMAX = 8
MARGIN = CMAX + 1
EPSILON = 1e-05

LANES = 128
STEP = 64
EDGE = 16
WINDOW = STEP + 2 * EDGE
SEGMENT = 32
PACKED = STEP // KZ
BX = LX // KX
BY = LY // KY
GROUPS = BX * BY
NX = LX + 2 * MARGIN
NY = LY + 2 * EDGE
KROWS = 8 + 2 * LY + 8
CELLS = KX * KY * KZ
CHUNK = 256


def pieces_of(value):
    high = lax.reduce_precision(value, 8, 7)
    middle = lax.reduce_precision(value - high, 8, 7)
    low = value - high - middle
    return [part.astype(jnp.bfloat16) for part in (high, middle, low)]


def track(
    choice,
    shift,
    own,
    kept,
    received,
    migration,
    column_gain,
    depth_gain,
    shift_cells,
    scores,
    displacement,
    samples,
    volume,
    kernels,
    sums,
):
    part = pl.program_id(0)
    blocks = own.shape[0]

    samples[...] = jnp.zeros(samples.shape, jnp.bfloat16)
    keep = choice[0] == 1
    for block in range(blocks):
        lanes = slice(block * LANES, (block + 1) * LANES)
        for j in range(PACKED):
            samples[j * SEGMENT : j * SEGMENT + KZ, lanes] = own[
                block, EDGE + j * KZ : EDGE + (j + 1) * KZ, :
            ]

    @pl.when(keep)
    def _():
        for block in range(blocks):
            lanes = slice(block * LANES, (block + 1) * LANES)
            samples[LANES : LANES + WINDOW, lanes] = kept[block]

    @pl.when(jnp.logical_not(keep))
    def _():
        for block in range(blocks):
            lanes = slice(block * LANES, (block + 1) * LANES)
            samples[LANES : LANES + WINDOW, lanes] = received[block]

    lane = lax.broadcasted_iota(jnp.int32, (8, LANES), 1)
    depth_row = jnp.broadcast_to(depth_gain[0], (8, LANES))
    own_row = pltpu.roll(depth_row, LANES - EDGE, 1)
    for j in range(1, PACKED):
        moved = pltpu.roll(depth_row, (j * KZ - EDGE) % LANES, 1)
        own_row = jnp.where(lane >= j * SEGMENT, moved, own_row)
    columns = jnp.transpose(column_gain[...])

    zero = jnp.zeros((NY, LANES), jnp.float32)
    for x in list(range(MARGIN)) + list(range(LX + MARGIN, NX)):
        volume[x * NY : (x + 1) * NY, :] = zero
    for x in range(LX):
        base = (x + MARGIN) * NY
        volume[base : base + EDGE, :] = zero[:EDGE]
        volume[base + EDGE + LY : base + NY, :] = zero[:EDGE]
        for by in range(BY + 1):
            kernels[x * KROWS + by * 16 : x * KROWS + by * 16 + 8, :] = zero[:8]

    right = samples[...]
    for chunk in range(LX * LY // CHUNK):
        raw = lax.dot_general(
            migration[chunk * CHUNK : (chunk + 1) * CHUNK, :],
            right,
            (((1,), (1,)), ((), ())),
            preferred_element_type=jnp.float32,
        )
        for piece in range(CHUNK // LY):
            x = chunk * (CHUNK // LY) + piece
            row = x * LY
            gain = columns[row % LANES : row % LANES + LY, row // LANES : row // LANES + 1]
            gain = jnp.broadcast_to(gain, (LY, LANES))
            mine = raw[piece * LY : (piece + 1) * LY, :LANES]
            reference = raw[piece * LY : (piece + 1) * LY, LANES:]
            mine = (mine * gain) * own_row[:1]
            reference = (reference * gain) * depth_row[:1]
            mine = mine.astype(jnp.bfloat16).astype(jnp.float32)
            reference = reference.astype(jnp.bfloat16).astype(jnp.float32)
            base = (x + MARGIN) * NY + EDGE
            volume[base : base + LY, :] = reference
            for by in range(BY):
                row = x * KROWS + 8 + by * 16
                kernels[row : row + 8, :] = mine[by * KY : (by + 1) * KY]

    place = lax.broadcasted_iota(jnp.int32, (8, LANES), 1)
    place = (place + 8) % LANES // SEGMENT
    segment = [place == j for j in range(PACKED)]
    row_number = lax.broadcasted_iota(jnp.int32, (8, LANES), 0)

    def group(g, carry):
        bx = g // BY
        by = g % BY
        starts = []
        turns = []
        for j in range(PACKED):
            bz = part * PACKED + j
            first = bx * KX + MARGIN + shift[0, 0, bx, by, bz]
            second = by * KY + EDGE + shift[1, 0, bx, by, bz]
            starts.append(first * NY + second)
            turns.append((j * KZ - EDGE + 2 * LANES - shift[2, 0, bx, by, bz]) % LANES)

        def gather(offset, stride):
            value = None
            for j in range(PACKED):
                start = starts[j] + offset
                if stride == 1:
                    rows = volume[pl.ds(start, 8), :]
                else:
                    rows = volume[pl.ds(start, 8, stride=stride), :]
                rows = pltpu.roll(rows, turns[j], 1)
                value = rows if value is None else jnp.where(segment[j], rows, value)
            return value

        base = bx * KX * KROWS + by * 16 + 8
        window = [gather((x - 1) * NY, 1) for x in range(KX + 2)]
        square = [value * value for value in window]
        middle = square[2]
        for x in range(3, KX):
            middle = middle + square[x]
        pair_low = square[0] + square[1]
        pair_high = square[KX] + square[KX + 1]
        center = middle + (square[1] + square[KX])
        cross = [None] * 7
        power = None

        def add(index, value):
            cross[index] = value if cross[index] is None else cross[index] + value

        for x in range(KX):
            row = base + x * KROWS
            kernel = kernels[pl.ds(row, 8), :]
            add(0, kernel * window[x + 1])
            add(1, kernel * window[x])
            add(2, kernel * window[x + 2])
            add(3, kernels[pl.ds(row + 1, 8), :] * window[x + 1])
            add(4, kernels[pl.ds(row - 1, 8), :] * window[x + 1])
            add(5, pltpu.roll(kernel, LANES - 1, 1) * window[x + 1])
            add(6, pltpu.roll(kernel, 1, 1) * window[x + 1])
            power = kernel * kernel if power is None else power + kernel * kernel
        before = gather(-1, NY)
        after = gather(KY, NY)
        add(3, kernels[pl.ds(base, 8, stride=KROWS), :] * before)
        add(4, kernels[pl.ds(base + KY - 1, 8, stride=KROWS), :] * after)
        low = jnp.where(row_number < KY - 1, center, 0.0) + before * before
        high = jnp.where(row_number > 0, center, 0.0) + after * after
        held = cross + [center, middle + pair_low, middle + pair_high, low, high, power]
        for index, value in enumerate(held):
            sums[index, pl.ds(g * 8, 8), :] = value
        return carry

    lax.fori_loop(0, GROUPS, group, 0)

    def total(index, bx):
        value = None
        for y in range(KY):
            rows = sums[index, pl.ds(bx * BY * 8 + y, BY, stride=8), :]
            value = rows if value is None else value + rows
        for width in (1, 2, 4, 8):
            value = value + pltpu.roll(value, LANES - width, 1)
        return value

    def compress(value):
        result = value
        for j in range(1, PACKED):
            result = jnp.where(lane == j, pltpu.roll(value, LANES - j * (SEGMENT - 1), 1), result)
        return result[:, :PACKED]

    for bx in range(BX):
        cross = [total(index, bx) for index in range(7)]
        cross[5] = pltpu.roll(cross[5], 1, 1)
        cross[6] = pltpu.roll(cross[6], LANES - 1, 1)
        center = total(7, bx)
        powers = [center] + [total(index, bx) for index in range(8, 12)]
        powers += [pltpu.roll(center, 1, 1), pltpu.roll(center, LANES - 1, 1)]
        kernel_power = total(12, bx) * (1.0 / CELLS) + EPSILON
        result = []
        for index in range(7):
            mean = cross[index] * (1.0 / CELLS)
            window_power = powers[index] * (1.0 / CELLS) + EPSILON
            result.append(
                compress(math.sqrt(CELLS) * mean / jnp.sqrt(kernel_power * window_power))
            )
            scores[index, 0, bx] = result[index]
        for axis in range(3):
            lower = result[1 + 2 * axis]
            upper = result[2 + 2 * axis]
            curvature = jnp.maximum(2.0 * result[0] - lower - upper, 1.0)
            cells = shift_cells[axis, 0, bx].astype(jnp.float32)
            displacement[axis, 0, bx] = cells + (upper - lower) / (2.0 * curvature)


def per_device(element_data, migration, column_gain, depth_gain, coarse_shift, reference_frame):
    elements_here, _, depth = element_data.shape
    depth_here = depth_gain.shape[0]
    slabs = lax.axis_size("slab")
    frames = lax.axis_size("frame")
    parts = depth_here // STEP
    chosen = reference_frame[0]
    frame = lax.axis_index("frame")
    slab = lax.axis_index("slab")

    turned = jnp.pad(element_data[:, 0, :].T, ((EDGE, EDGE), (0, 0)))
    ends = jnp.concatenate([depth_gain[:MARGIN], depth_gain[depth_here - MARGIN :]])
    note = jnp.concatenate(pieces_of(ends))
    note_rows = -(-note.shape[0] // elements_here)
    note = jnp.pad(note, (0, note_rows * elements_here - note.shape[0]))
    note = note.reshape(note_rows, elements_here)
    windows = []
    for number in range(depth // STEP):
        window = turned[number * STEP : number * STEP + WINDOW]
        if number % parts == 0:
            window = jnp.concatenate([note, window[note_rows:]])
        windows.append(window)
    windows = jnp.stack(windows).reshape(slabs, parts * WINDOW, elements_here)
    own = lax.all_to_all(windows, "slab", split_axis=0, concat_axis=0, tiled=True)

    notes = own[:, :note_rows, :].reshape(slabs, -1)[:, : 6 * MARGIN].astype(jnp.float32)
    notes = notes.reshape(slabs, 3, 2 * MARGIN)
    notes = notes[:, 0] + notes[:, 1] + notes[:, 2]
    before = lax.dynamic_index_in_dim(notes, (slab - 1) % slabs, 0, keepdims=False)[MARGIN:]
    after = lax.dynamic_index_in_dim(notes, (slab + 1) % slabs, 0, keepdims=False)[:MARGIN]
    spare = jnp.ones((EDGE - MARGIN,), jnp.float32)
    extended = jnp.concatenate([spare, before, depth_gain, after, spare])
    gains = jnp.stack(
        [jnp.pad(extended[i * STEP : i * STEP + WINDOW], (0, LANES - WINDOW)) for i in range(parts)]
    ).reshape(parts, 1, LANES)

    if elements_here != LANES:
        own = own.transpose(1, 0, 2).reshape(parts * WINDOW, -1, LANES).transpose(1, 0, 2)

    kept = own
    received = own
    bit = 1
    while bit < frames:
        if bit > 1:
            mine = (chosen ^ frame) & (bit - 1 & ~(bit // 2 - 1)) == 0
            kept = jnp.where(mine, kept, received)
        received = lax.ppermute(kept, "frame", [(i, i ^ bit) for i in range(frames)])
        bit *= 2
    choice = ((chosen ^ frame) & (frames // 2) == 0).astype(jnp.int32).reshape(1)

    blocks = own.shape[0]
    piece = pl.BlockSpec((blocks, WINDOW, LANES), lambda i: (0, i, 0))
    cells = coarse_shift.shape[:4] + (PACKED,)
    if parts == 1:
        shift_vector = coarse_shift
        vector = lambda n: pl.BlockSpec((n,) + coarse_shift.shape[1:], lambda i: (0, 0, 0, 0, 0))
        shapes = [(n,) + coarse_shift.shape[1:] for n in (7, 3)]
    else:
        shift_vector = coarse_shift.reshape(coarse_shift.shape[:4] + (parts, PACKED))
        shift_vector = jnp.moveaxis(shift_vector, 4, 0).reshape((parts * 3,) + cells[1:])
        vector = lambda n: pl.BlockSpec((n,) + cells[1:], lambda i: (i, 0, 0, 0, 0))
        shapes = [(parts * n,) + cells[1:] for n in (7, 3)]
    whole = lambda array: pl.BlockSpec(array.shape, lambda i: (0,) * array.ndim)
    gain_table = column_gain.reshape(-1, LANES)
    scores, displacement = pl.pallas_call(
        track,
        grid=(parts,),
        in_specs=[
            pl.BlockSpec(memory_space=pltpu.SMEM),
            pl.BlockSpec(memory_space=pltpu.SMEM),
            piece,
            piece,
            piece,
            whole(migration),
            whole(gain_table),
            pl.BlockSpec((1, 1, LANES), lambda i: (i, 0, 0)),
            vector(3),
        ],
        out_specs=[vector(7), vector(3)],
        out_shape=[jax.ShapeDtypeStruct(shape, jnp.float32) for shape in shapes],
        scratch_shapes=[
            pltpu.VMEM((2 * LANES, blocks * LANES), jnp.bfloat16),
            pltpu.VMEM((NX * NY, LANES), jnp.float32),
            pltpu.VMEM((LX * KROWS, LANES), jnp.float32),
            pltpu.VMEM((13, GROUPS * 8, LANES), jnp.float32),
        ],
        name="track",
    )(
        choice,
        coarse_shift,
        own,
        kept,
        received,
        migration,
        gain_table,
        gains,
        shift_vector,
    )
    if parts > 1:
        scores, displacement = (
            jnp.moveaxis(array.reshape((parts, -1) + cells[1:]), 0, 4).reshape(
                (array.shape[0] // parts,) + coarse_shift.shape[1:]
            )
            for array in (scores, displacement)
        )
    return scores, displacement


def solution(mesh):
    blocks = P(None, "frame", None, None, "slab")
    placed = (P("slab", "frame", None), P(), P(), P("slab"), blocks, P())
    return jax.shard_map(
        per_device, mesh=mesh, in_specs=placed, out_specs=(blocks, blocks), check_vma=False
    )
```

```python
import functools
import math

import jax
import jax.numpy as jnp
from jax import lax
from jax.experimental import pallas as pl
from jax.experimental.pallas import tpu as pltpu
from jax.sharding import PartitionSpec as P

LX = 32
LY = 64
KX = 8
KY = 8
KZ = 16
CMAX = 8
MARGIN = CMAX + 1
EPSILON = 1e-05

LANES = 128
STEP = 64
EDGE = 16
WINDOW = STEP + 2 * EDGE
SEGMENT = 32
PACKED = STEP // KZ
BX = LX // KX
BY = LY // KY
GROUPS = BX * BY
NX = LX + 2 * MARGIN
NY = LY + 2 * EDGE
KROWS = 8 + 2 * LY + 8
CELLS = KX * KY * KZ
CHUNK = 256


def pieces_of(value):
    high = value.astype(jnp.bfloat16).astype(jnp.float32)
    middle = (value - high).astype(jnp.bfloat16).astype(jnp.float32)
    return high, middle, value - high - middle


def window_rows(element_data, depth_gain, windows, row):
    row[...] = jnp.zeros(row.shape, jnp.float32)
    for index, piece in enumerate(pieces_of(depth_gain[...])):
        row[index : index + 1, :STEP] = piece
    note = row[...].astype(jnp.bfloat16)
    slabs = windows.shape[0]
    empty = jnp.zeros((EDGE, LANES), jnp.bfloat16)
    spare = lax.broadcasted_iota(jnp.int32, (EDGE, LANES), 0) < 3

    def put(slab, first, rows):
        if 0 <= slab < slabs:
            if first == 0:
                rows = jnp.where(spare, note, rows)
            windows[slab, first : first + EDGE, :] = rows

    put(0, 0, empty)
    put(slabs - 1, EDGE + STEP, empty)
    for column in range(element_data.shape[1] // LANES):
        turned = jnp.transpose(element_data[:, column * LANES : (column + 1) * LANES])
        for unit in range(LANES // EDGE):
            slab, place = divmod(column * LANES + unit * EDGE, STEP)
            rows = turned[unit * EDGE : (unit + 1) * EDGE]
            put(slab, place + EDGE, rows)
            if place == STEP - EDGE:
                put(slab + 1, 0, rows)
            if place == 0:
                put(slab - 1, EDGE + STEP, rows)


def depth_row(choice, samples):
    lane = lax.broadcasted_iota(jnp.int32, (8, LANES), 1)

    def of(which):
        note = samples[choice[which], :EDGE, :].astype(jnp.float32)
        return jnp.broadcast_to(note[0:1] + note[1:2] + note[2:3], (8, LANES))

    row = pltpu.roll(of(2), EDGE, 1)
    row = jnp.where(lane < EDGE, pltpu.roll(of(1), (EDGE - STEP) % LANES, 1), row)
    return jnp.where(lane >= EDGE + STEP, pltpu.roll(of(3), EDGE + STEP, 1), row)


def migrate(right, migration, columns, gains, store):
    for chunk in range(LX * LY // CHUNK):
        raw = lax.dot_general(
            migration[chunk * CHUNK : (chunk + 1) * CHUNK, :],
            right,
            (((1,), (1,)), ((), ())),
            preferred_element_type=jnp.float32,
        )
        for piece in range(CHUNK // LY):
            x = chunk * (CHUNK // LY) + piece
            row = x * LY
            gain = columns[row % LANES : row % LANES + LY, row // LANES : row // LANES + 1]
            image = (raw[piece * LY : (piece + 1) * LY] * jnp.broadcast_to(gain, (LY, LANES))) * gains
            store(x, image.astype(jnp.bfloat16).astype(jnp.float32))


def own_kernels(choice, own, migration, column_gain, kernels):
    gap = jnp.zeros((SEGMENT - KZ, migration.shape[1]), jnp.bfloat16)
    rows = []
    for j in range(PACKED):
        pieces = [own[b, EDGE + j * KZ : EDGE + (j + 1) * KZ, :] for b in range(own.shape[0])]
        rows += [jnp.concatenate(pieces, axis=1), gap]
    lane = lax.broadcasted_iota(jnp.int32, (8, LANES), 1)
    note = own[choice[2], :EDGE, :].astype(jnp.float32)
    row = jnp.broadcast_to(note[0:1] + note[1:2] + note[2:3], (8, LANES))
    gains = row
    for j in range(1, PACKED):
        gains = jnp.where(lane >= j * SEGMENT, pltpu.roll(row, j * KZ, 1), gains)
    for x in range(LX):
        for by in range(BY + 1):
            kernels[x * KROWS + by * 16 : x * KROWS + by * 16 + 8, :] = jnp.zeros((8, LANES))

    def store(x, image):
        for by in range(BY):
            row = x * KROWS + 8 + by * 16
            kernels[row : row + 8, :] = image[by * KY : (by + 1) * KY]

    migrate(
        jnp.concatenate(rows), migration, jnp.transpose(column_gain[...]), gains[:1], store
    )


def track(
    choice,
    shift,
    kept,
    received,
    migration,
    column_gain,
    kernels,
    shift_cells,
    scores,
    displacement,
    volume,
    sums,
    turned,
):
    keep = choice[0] == 1
    zero = jnp.zeros((NY, LANES), jnp.float32)
    for x in list(range(MARGIN)) + list(range(LX + MARGIN, NX)):
        volume[x * NY : (x + 1) * NY, :] = zero
    for x in range(LX):
        base = (x + MARGIN) * NY
        volume[base : base + EDGE, :] = zero[:EDGE]
        volume[base + EDGE + LY : base + NY, :] = zero[:EDGE]

    def store(x, image):
        base = (x + MARGIN) * NY + EDGE
        volume[base : base + LY, :] = image

    pieces = [jnp.where(keep, kept[b], received[b]) for b in range(kept.shape[0])]
    spare = jnp.zeros((LANES - WINDOW, migration.shape[1]), jnp.bfloat16)
    right = jnp.concatenate([jnp.concatenate(pieces, axis=1), spare])
    columns = jnp.transpose(column_gain[...])
    migrate(right, migration, columns, depth_row(choice, kept)[:1], store)

    place = lax.broadcasted_iota(jnp.int32, (8, LANES), 1)
    place = (place + 8) % LANES // SEGMENT
    segment = [place == j for j in range(PACKED)]
    row_number = lax.broadcasted_iota(jnp.int32, (8, LANES), 0)

    def group(g, carry):
        bx = g // BY
        by = g % BY
        starts = []
        turns = []
        for j in range(PACKED):
            first = bx * KX + MARGIN + shift[0, 0, bx, j, by]
            second = by * KY + EDGE + shift[1, 0, bx, j, by]
            starts.append(first * NY + second)
            turns.append((j * KZ - EDGE + 2 * LANES - shift[2, 0, bx, j, by]) % LANES)

        def gather(offset, stride):
            value = None
            for j in range(PACKED):
                start = starts[j] + offset
                if stride == 1:
                    rows = volume[pl.ds(start, 8), :]
                else:
                    rows = volume[pl.ds(start, 8, stride=stride), :]
                rows = pltpu.roll(rows, turns[j], 1)
                value = rows if value is None else jnp.where(segment[j], rows, value)
            return value

        base = bx * KX * KROWS + by * 16 + 8
        window = [gather((x - 1) * NY, 1) for x in range(KX + 2)]
        square = [value * value for value in window]
        middle = square[2]
        for x in range(3, KX):
            middle = middle + square[x]
        pair_low = square[0] + square[1]
        pair_high = square[KX] + square[KX + 1]
        center = middle + (square[1] + square[KX])
        cross = [None] * 7
        power = None

        def add(index, value):
            cross[index] = value if cross[index] is None else cross[index] + value

        for x in range(KX):
            row = base + x * KROWS
            kernel = kernels[pl.ds(row, 8), :]
            add(0, kernel * window[x + 1])
            add(1, kernel * window[x])
            add(2, kernel * window[x + 2])
            add(3, kernels[pl.ds(row + 1, 8), :] * window[x + 1])
            add(4, kernels[pl.ds(row - 1, 8), :] * window[x + 1])
            add(5, pltpu.roll(kernel, LANES - 1, 1) * window[x + 1])
            add(6, pltpu.roll(kernel, 1, 1) * window[x + 1])
            power = kernel * kernel if power is None else power + kernel * kernel
        before = gather(-1, NY)
        after = gather(KY, NY)
        add(3, kernels[pl.ds(base, 8, stride=KROWS), :] * before)
        add(4, kernels[pl.ds(base + KY - 1, 8, stride=KROWS), :] * after)
        low = jnp.where(row_number < KY - 1, center, 0.0) + before * before
        high = jnp.where(row_number > 0, center, 0.0) + after * after
        held = cross[:5] + [center, middle + pair_low, middle + pair_high]
        held += [low, high, power, cross[5], cross[6]]
        for index, value in enumerate(held):
            sums[index, pl.ds(g * 8, 8), :] = value
        return carry

    lax.fori_loop(0, GROUPS, group, 0)

    def rows_of(index):
        parts = []
        for bx in range(BX):
            value = None
            for y in range(KY):
                rows = sums[index, pl.ds(bx * BY * 8 + y, BY, stride=8), :]
                value = rows if value is None else value + rows
            parts.append(value)
        return parts

    row_of_block = lax.broadcasted_iota(jnp.int32, (8, LANES), 0)

    def totals(block, offsets):
        value = jnp.transpose(jnp.concatenate([part for index in block for part in rows_of(index)]))
        turned[0:8, :] = value[LANES - 8 :]
        turned[8 : LANES + 8, :] = value
        turned[LANES + 8 : LANES + 16, :] = value[:8]
        result = []
        for offset in offsets:
            total = None
            for j in range(PACKED):
                row = 8 + j * SEGMENT + offset
                value = turned[row : row + 8, :] + turned[row + 8 : row + 16, :]
                value = jnp.broadcast_to(jnp.sum(value, axis=0, keepdims=True), (8, LANES))
                total = value if total is None else jnp.where(row_of_block >= j, value, total)
            result.append(total)
        return result

    def lanes_of(value, place):
        return value if place == 0 else pltpu.roll(value, LANES - place * GROUPS, 1)

    (first,) = totals((0, 1, 2, 3), (0,))
    second, second_low, second_high = totals((4, 5, 6, 7), (0, -1, 1))
    third, third_low, third_high = totals((8, 9, 10, 11), (0, -1, 1))
    (fourth,) = totals((12, 12, 12, 12), (1,))
    cross = [lanes_of(first, place) for place in range(4)]
    cross += [second, lanes_of(third_low, 3), fourth]
    powers = [lanes_of(second, place) for place in (1, 2, 3)]
    powers += [third, lanes_of(third, 1), lanes_of(second_low, 1), lanes_of(second_high, 1)]
    kernel_power = lanes_of(third, 2) * (1.0 / CELLS) + EPSILON
    result = []
    for index in range(7):
        mean = cross[index] * (1.0 / CELLS)
        window_power = powers[index] * (1.0 / CELLS) + EPSILON
        result.append(math.sqrt(CELLS) * mean / jnp.sqrt(kernel_power * window_power))
    moves = []
    for axis in range(3):
        lower = result[1 + 2 * axis]
        upper = result[2 + 2 * axis]
        curvature = jnp.maximum(2.0 * result[0] - lower - upper, 1.0)
        moves.append((upper - lower) / (2.0 * curvature))
    for bx in range(BX):
        for index in range(7):
            value = pltpu.roll(result[index], (LANES - bx * BY) % LANES, 1)
            scores[index, 0, bx] = value[:PACKED, :BY]
        for axis in range(3):
            value = pltpu.roll(moves[axis], (LANES - bx * BY) % LANES, 1)
            cells = shift_cells[axis, 0, bx].astype(jnp.float32)
            displacement[axis, 0, bx] = cells + value[:PACKED, :BY]


def on_chip(count):
    return [pl.BlockSpec(memory_space=pltpu.VMEM)] * count


def per_device(element_data, migration, column_gain, depth_gain, coarse_shift, reference_frame):
    elements_here, frames_here, depth = element_data.shape
    depth_here = depth_gain.shape[0]
    slabs = lax.axis_size("slab")
    frames = lax.axis_size("frame")
    elements = elements_here * slabs
    assert frames_here == 1 and depth_here == STEP
    chosen = reference_frame[0]
    frame = lax.axis_index("frame")
    slab = lax.axis_index("slab")
    own_data = element_data.reshape(elements_here, depth)

    if elements_here == LANES:
        windows = pl.pallas_call(
            window_rows,
            in_specs=on_chip(2),
            out_specs=on_chip(1)[0],
            out_shape=jax.ShapeDtypeStruct((slabs, WINDOW, LANES), jnp.bfloat16),
            scratch_shapes=[pltpu.VMEM((EDGE, LANES), jnp.float32)],
            name="window_rows",
        )(own_data, depth_gain.reshape(1, STEP))
        own = lax.all_to_all(windows, "slab", split_axis=0, concat_axis=0, tiled=True)
        places = [(slab - 1) % slabs, slab, (slab + 1) % slabs]
    else:
        turned = jnp.pad(own_data.T, ((EDGE, EDGE), (0, 0)))
        windows = jnp.stack([turned[i * STEP : i * STEP + WINDOW] for i in range(slabs)])
        own = lax.all_to_all(windows, "slab", split_axis=0, concat_axis=0, tiled=True)
        own = own.transpose(1, 0, 2).reshape(WINDOW, elements // LANES, LANES).transpose(1, 0, 2)
        ring = [(i, (i + 1) % slabs) for i in range(slabs)]
        left = lax.ppermute(depth_gain, "slab", ring)
        right = lax.ppermute(depth_gain, "slab", [(j, i) for i, j in ring])
        high = lambda value: lax.reduce_precision(value, 8, 7)
        for place, value in enumerate((left, depth_gain, right)):
            middle = high(value - high(value))
            note = jnp.stack([high(value), middle, value - high(value) - middle])
            own = own.at[place, :3, :STEP].set(note.astype(jnp.bfloat16))
        places = [0, 1, 2]

    kept = own
    received = own
    bit = 1
    while bit < frames:
        if bit > 1:
            mine = (chosen ^ frame) & (bit // 2) == 0
            kept = jnp.where(mine, kept, received)
        received = lax.ppermute(kept, "frame", [(i, i ^ bit) for i in range(frames)])
        bit *= 2
    keep = ((chosen ^ frame) & (frames // 2) == 0).astype(jnp.int32)
    choice = jnp.stack([keep] + [jnp.asarray(place, jnp.int32) for place in places])

    gain_table = column_gain.reshape(-1, LANES)
    scalars = pl.BlockSpec(memory_space=pltpu.SMEM)
    kernels = pl.pallas_call(
        own_kernels,
        in_specs=[scalars] + on_chip(3),
        out_specs=on_chip(1)[0],
        out_shape=jax.ShapeDtypeStruct((LX * KROWS, LANES), jnp.float32),
        name="own_kernels",
    )(choice, own, migration, gain_table)

    turn = (0, 1, 2, 4, 3)
    shifts = coarse_shift.transpose(turn)
    shapes = [jax.ShapeDtypeStruct((n,) + shifts.shape[1:], jnp.float32) for n in (7, 3)]
    scores, displacement = pl.pallas_call(
        track,
        in_specs=[scalars, scalars] + on_chip(6),
        out_specs=on_chip(2),
        out_shape=shapes,
        scratch_shapes=[
            pltpu.VMEM((NX * NY, LANES), jnp.float32),
            pltpu.VMEM((13, GROUPS * 8, LANES), jnp.float32),
            pltpu.VMEM((LANES + 16, LANES), jnp.float32),
        ],
        name="track",
    )(choice, shifts, kept, received, migration, gain_table, kernels, shifts)
    return scores.transpose(turn), displacement.transpose(turn)


def solution(mesh):
    blocks = P(None, "frame", None, None, "slab")
    placed = (P("slab", "frame", None), P(), P(), P("slab"), blocks, P())
    return jax.shard_map(
        per_device, mesh=mesh, in_specs=placed, out_specs=(blocks, blocks), check_vma=False
    )
```

```python
import functools
import math

import jax
import jax.numpy as jnp
from jax import lax
from jax.experimental import pallas as pl
from jax.experimental.pallas import tpu as pltpu
from jax.sharding import PartitionSpec as P

LX = 32
LY = 64
KX = 8
KY = 8
KZ = 16
CMAX = 8
MARGIN = CMAX + 1
EPSILON = 1e-05

LANES = 128
STEP = 64
EDGE = 16
WINDOW = STEP + 2 * EDGE
SEGMENT = 32
PACKED = STEP // KZ
BX = LX // KX
BY = LY // KY
GROUPS = BX * BY
NX = LX + 2 * MARGIN
NY = 89
KROWS = 145
SPREAD = LX * KROWS + 7
VOLUME = NX * NY + 6
SUMS = 9
CELLS = KX * KY * KZ
CHUNK = 256
UNROLL = 32


def pieces_of(value):
    high = value.astype(jnp.bfloat16).astype(jnp.float32)
    middle = (value - high).astype(jnp.bfloat16).astype(jnp.float32)
    return high, middle, value - high - middle


def window_rows(element_data, depth_gain, windows, row):
    row[...] = jnp.zeros(row.shape, jnp.float32)
    for index, piece in enumerate(pieces_of(depth_gain[...])):
        row[index : index + 1, :STEP] = piece
    note = row[...].astype(jnp.bfloat16)
    slabs = windows.shape[0]
    empty = jnp.zeros((EDGE, LANES), jnp.bfloat16)
    spare = lax.broadcasted_iota(jnp.int32, (EDGE, LANES), 0) < 3

    def put(slab, first, rows):
        if 0 <= slab < slabs:
            if first == 0:
                rows = jnp.where(spare, note, rows)
            windows[slab, first : first + EDGE, :] = rows

    put(0, 0, empty)
    put(slabs - 1, EDGE + STEP, empty)
    for column in range(element_data.shape[1] // LANES):
        turned = jnp.transpose(element_data[:, column * LANES : (column + 1) * LANES])
        for unit in range(LANES // EDGE):
            slab, place = divmod(column * LANES + unit * EDGE, STEP)
            rows = turned[unit * EDGE : (unit + 1) * EDGE]
            put(slab, place + EDGE, rows)
            if place == STEP - EDGE:
                put(slab + 1, 0, rows)
            if place == 0:
                put(slab - 1, EDGE + STEP, rows)


def depth_row(choice, samples):
    lane = lax.broadcasted_iota(jnp.int32, (8, LANES), 1)

    def of(which):
        note = samples[choice[which], :EDGE, :].astype(jnp.float32)
        return jnp.broadcast_to(note[0:1] + note[1:2] + note[2:3], (8, LANES))

    row = pltpu.roll(of(2), EDGE, 1)
    row = jnp.where(lane < EDGE, pltpu.roll(of(1), (EDGE - STEP) % LANES, 1), row)
    return jnp.where(lane >= EDGE + STEP, pltpu.roll(of(3), EDGE + STEP, 1), row)


def migrate(right, migration, columns, gains, store):
    for chunk in range(LX * LY // CHUNK):
        raw = lax.dot_general(
            migration[chunk * CHUNK : (chunk + 1) * CHUNK, :],
            right,
            (((1,), (1,)), ((), ())),
            preferred_element_type=jnp.float32,
        )
        for piece in range(CHUNK // LY):
            x = chunk * (CHUNK // LY) + piece
            row = x * LY
            gain = columns[row % LANES : row % LANES + LY, row // LANES : row // LANES + 1]
            image = (raw[piece * LY : (piece + 1) * LY] * jnp.broadcast_to(gain, (LY, LANES))) * gains
            store(x, image.astype(jnp.bfloat16).astype(jnp.float32))


def own_kernels(
    choice, own, migration, column_gain, kernels, deeper, shallower, edges, powers
):
    gap = jnp.zeros((SEGMENT - KZ, migration.shape[1]), jnp.bfloat16)
    rows = []
    for j in range(PACKED):
        pieces = [own[b, EDGE + j * KZ : EDGE + (j + 1) * KZ, :] for b in range(own.shape[0])]
        rows += [jnp.concatenate(pieces, axis=1), gap]
    lane = lax.broadcasted_iota(jnp.int32, (8, LANES), 1)
    note = own[choice[2], :EDGE, :].astype(jnp.float32)
    row = jnp.broadcast_to(note[0:1] + note[1:2] + note[2:3], (8, LANES))
    gains = row
    for j in range(1, PACKED):
        gains = jnp.where(lane >= j * SEGMENT, pltpu.roll(row, j * KZ, 1), gains)
    for x in range(LX):
        for by in range(BY + 1):
            kernels[x * KROWS + by * 16 : x * KROWS + by * 16 + 8, :] = jnp.zeros((8, LANES))

    def store(x, image):
        for by in range(BY):
            row = x * KROWS + 8 + by * 16
            kernel = image[by * KY : (by + 1) * KY]
            kernels[row : row + 8, :] = kernel
            row = x * LY + by * KY
            shallower[row : row + 8, :] = pltpu.roll(kernel, LANES - 1, 1)
            deeper[row : row + 8, :] = pltpu.roll(kernel, 1, 1)

    migrate(
        jnp.concatenate(rows), migration, jnp.transpose(column_gain[...]), gains[:1], store
    )
    for g in range(GROUPS):
        base = g // BY * KX * KROWS + g % BY * 16 + 8
        power = None
        for x in range(KX):
            kernel = kernels[base + x * KROWS : base + x * KROWS + 8, :]
            power = kernel * kernel if power is None else power + kernel * kernel
        powers[g * SUMS : g * SUMS + 8, :] = power
        for index, row in enumerate((base, base + KY - 1)):
            edges[index, g * 8 : g * 8 + 8, :] = kernels[pl.ds(row, 8, stride=KROWS), :]


def track(
    choice,
    shift,
    kept,
    received,
    migration,
    column_gain,
    kernels,
    deeper,
    shallower,
    edges,
    kernel_powers,
    shift_cells,
    scores,
    displacement,
    volume,
    sums,
    turned,
):
    keep = choice[0] == 1
    zero = jnp.zeros((NY, LANES), jnp.float32)
    for x in list(range(MARGIN)) + list(range(LX + MARGIN, NX)):
        volume[x * NY : (x + 1) * NY, :] = zero
    for x in range(MARGIN, LX + MARGIN):
        volume[x * NY : x * NY + MARGIN, :] = zero[:MARGIN]
        volume[x * NY + MARGIN + LY : (x + 1) * NY, :] = zero[: NY - MARGIN - LY]

    def store(x, image):
        base = (x + MARGIN) * NY + MARGIN
        volume[base : base + LY, :] = image

    pieces = [jnp.where(keep, kept[b], received[b]) for b in range(kept.shape[0])]
    spare = jnp.zeros((LANES - WINDOW, migration.shape[1]), jnp.bfloat16)
    right = jnp.concatenate([jnp.concatenate(pieces, axis=1), spare])
    columns = jnp.transpose(column_gain[...])
    migrate(right, migration, columns, depth_row(choice, kept)[:1], store)

    place = lax.broadcasted_iota(jnp.int32, (16, LANES), 1)
    segment = [((place + 8) & (LANES - 1)) // SEGMENT == j for j in range(PACKED)]
    row_number = lax.broadcasted_iota(jnp.int32, (8, LANES), 0)

    def group(g, carry):
        bx = g // BY
        by = g & (BY - 1)
        starts = []
        turns = []
        for j in range(PACKED):
            first = bx * KX + MARGIN + shift[0, 0, bx, j, by]
            second = by * KY + MARGIN + shift[1, 0, bx, j, by]
            starts.append(first * NY + second)
            turns.append((j * KZ - EDGE + LANES - shift[2, 0, bx, j, by]) & (LANES - 1))

        def gather(offsets, stride=None):
            value = None
            for j in range(PACKED):
                pair = []
                for offset in offsets:
                    if stride is None:
                        pair.append(volume[pl.ds(starts[j] + offset, 8), :])
                    else:
                        pair.append(volume[pl.ds(starts[j] + offset, 8, stride=stride), :])
                rows = jnp.concatenate(pair).astype(jnp.bfloat16)
                rows = pltpu.roll(rows, turns[j], 1)
                value = rows if value is None else jnp.where(segment[j], rows, value)
            value = value.astype(jnp.float32)
            return [value[:8], value[8:]]

        window = []
        for x in range(-1, KX, 2):
            window += gather((x * NY, (x + 1) * NY))
        before, after = gather((-1, KY), NY)
        square = [value * value for value in window]
        middle = square[2]
        for x in range(3, KX):
            middle = middle + square[x]
        pair_low = square[0] + square[1]
        pair_high = square[KX] + square[KX + 1]
        center = middle + (square[1] + square[KX])
        cross = [None] * 7

        def add(index, value):
            cross[index] = value if cross[index] is None else cross[index] + value

        base = bx * KX * KROWS + by * 16 + 8
        flat = bx * KX * LY + by * KY
        for x in range(KX):
            row = base + x * KROWS
            kernel = kernels[pl.ds(row, 8), :]
            add(0, kernel * window[x + 1])
            add(1, kernel * window[x])
            add(2, kernel * window[x + 2])
            add(3, kernels[pl.ds(row + 1, 8), :] * window[x + 1])
            add(4, kernels[pl.ds(row - 1, 8), :] * window[x + 1])
            aligned = pl.ds(pl.multiple_of(flat + x * LY, 8), 8)
            add(5, shallower[aligned, :] * window[x + 1])
            add(6, deeper[aligned, :] * window[x + 1])
        rows = pl.ds(pl.multiple_of(g * 8, 8), 8)
        add(3, edges[0, rows, :] * before)
        add(4, edges[1, rows, :] * after)
        low = jnp.where(row_number < KY - 1, center, 0.0) + before * before
        high = jnp.where(row_number > 0, center, 0.0) + after * after
        held = cross[:5] + [center, middle + pair_low, middle + pair_high]
        held += [low, high, cross[5], cross[6]]
        for index, value in enumerate(held):
            sums[index, pl.ds(g * SUMS, 8), :] = value
        return carry

    lax.fori_loop(0, GROUPS, group, 0, unroll=UNROLL)

    def rows_of(index):
        parts = []
        for bx in range(BX):
            value = None
            for y in range(KY):
                place = pl.ds(bx * BY * SUMS + y, BY, stride=SUMS)
                rows = sums[index, place, :] if index < 12 else kernel_powers[place, :]
                value = rows if value is None else value + rows
            parts.append(value)
        return parts

    row_of_block = lax.broadcasted_iota(jnp.int32, (8, LANES), 0)

    def totals(block, offsets):
        value = jnp.transpose(jnp.concatenate([part for index in block for part in rows_of(index)]))
        turned[0:8, :] = value[LANES - 8 :]
        turned[8 : LANES + 8, :] = value
        turned[LANES + 8 : LANES + 16, :] = value[:8]
        result = []
        for offset in offsets:
            total = None
            for j in range(PACKED):
                row = 8 + j * SEGMENT + offset
                value = turned[row : row + 8, :] + turned[row + 8 : row + 16, :]
                value = jnp.broadcast_to(jnp.sum(value, axis=0, keepdims=True), (8, LANES))
                total = value if total is None else jnp.where(row_of_block >= j, value, total)
            result.append(total)
        return result

    def lanes_of(value, place):
        return value if place == 0 else pltpu.roll(value, LANES - place * GROUPS, 1)

    (first,) = totals((0, 1, 2, 3), (0,))
    second, second_low, second_high = totals((4, 5, 6, 7), (0, -1, 1))
    third, third_low, third_high = totals((8, 9, 10, 11), (0, -1, 1))
    (fourth,) = totals((12, 12, 12, 12), (0,))
    cross = [lanes_of(first, place) for place in range(4)]
    cross += [second, lanes_of(third_low, 2), lanes_of(third_high, 3)]
    powers = [lanes_of(second, place) for place in (1, 2, 3)]
    powers += [third, lanes_of(third, 1), lanes_of(second_low, 1), lanes_of(second_high, 1)]
    kernel_power = fourth * (1.0 / CELLS) + EPSILON
    result = []
    for index in range(7):
        mean = cross[index] * (1.0 / CELLS)
        window_power = powers[index] * (1.0 / CELLS) + EPSILON
        result.append(math.sqrt(CELLS) * mean / jnp.sqrt(kernel_power * window_power))
    moves = []
    for axis in range(3):
        lower = result[1 + 2 * axis]
        upper = result[2 + 2 * axis]
        curvature = jnp.maximum(2.0 * result[0] - lower - upper, 1.0)
        moves.append((upper - lower) / (2.0 * curvature))
    for bx in range(BX):
        for index in range(7):
            value = pltpu.roll(result[index], (LANES - bx * BY) % LANES, 1)
            scores[index, 0, bx] = value[:PACKED, :BY]
        for axis in range(3):
            value = pltpu.roll(moves[axis], (LANES - bx * BY) % LANES, 1)
            cells = shift_cells[axis, 0, bx].astype(jnp.float32)
            displacement[axis, 0, bx] = cells + value[:PACKED, :BY]


def on_chip(count):
    return [pl.BlockSpec(memory_space=pltpu.VMEM)] * count


def pinned(array):
    return pltpu.with_memory_space_constraint(array, pltpu.VMEM)


def per_device(element_data, migration, column_gain, depth_gain, coarse_shift, reference_frame):
    elements_here, frames_here, depth = element_data.shape
    depth_here = depth_gain.shape[0]
    slabs = lax.axis_size("slab")
    frames = lax.axis_size("frame")
    elements = elements_here * slabs
    assert frames_here == 1 and depth_here == STEP
    chosen = reference_frame[0]
    frame = lax.axis_index("frame")
    slab = lax.axis_index("slab")
    own_data = element_data.reshape(elements_here, depth)

    if elements_here == LANES:
        windows = pl.pallas_call(
            window_rows,
            in_specs=on_chip(2),
            out_specs=on_chip(1)[0],
            out_shape=jax.ShapeDtypeStruct((slabs, WINDOW, LANES), jnp.bfloat16),
            scratch_shapes=[pltpu.VMEM((EDGE, LANES), jnp.float32)],
            compiler_params=pltpu.CompilerParams(vmem_limit_bytes=4 << 20),
            name="window_rows",
        )(own_data, depth_gain.reshape(1, STEP))
        own = lax.all_to_all(windows, "slab", split_axis=0, concat_axis=0, tiled=True)
        places = [(slab - 1) % slabs, slab, (slab + 1) % slabs]
    else:
        turned = jnp.pad(own_data.T, ((EDGE, EDGE), (0, 0)))
        windows = jnp.stack([turned[i * STEP : i * STEP + WINDOW] for i in range(slabs)])
        own = lax.all_to_all(windows, "slab", split_axis=0, concat_axis=0, tiled=True)
        own = own.transpose(1, 0, 2).reshape(WINDOW, elements // LANES, LANES).transpose(1, 0, 2)
        ring = [(i, (i + 1) % slabs) for i in range(slabs)]
        left = lax.ppermute(depth_gain, "slab", ring)
        right = lax.ppermute(depth_gain, "slab", [(j, i) for i, j in ring])
        high = lambda value: lax.reduce_precision(value, 8, 7)
        for place, value in enumerate((left, depth_gain, right)):
            middle = high(value - high(value))
            note = jnp.stack([high(value), middle, value - high(value) - middle])
            own = own.at[place, :3, :STEP].set(note.astype(jnp.bfloat16))
        places = [0, 1, 2]

    kept = own
    received = own
    bit = 1
    while bit < frames:
        if bit > 1:
            mine = (chosen ^ frame) & (bit // 2) == 0
            kept = jnp.where(mine, kept, received)
        received = lax.ppermute(kept, "frame", [(i, i ^ bit) for i in range(frames)])
        bit *= 2
    keep = ((chosen ^ frame) & (frames // 2) == 0).astype(jnp.int32)
    choice = jnp.stack([keep] + [jnp.asarray(place, jnp.int32) for place in places])

    gain_table = column_gain.reshape(-1, LANES)
    scalars = pl.BlockSpec(memory_space=pltpu.SMEM)
    own_shapes = [(SPREAD, LANES), (LX * LY, LANES), (LX * LY, LANES)]
    own_shapes += [(2, GROUPS * 8, LANES), (GROUPS * SUMS, LANES)]
    kernel_arrays = pl.pallas_call(
        own_kernels,
        in_specs=[scalars] + on_chip(3),
        out_specs=on_chip(5),
        out_shape=[pltpu.VMEM(shape, jnp.float32) for shape in own_shapes],
        compiler_params=pltpu.CompilerParams(vmem_limit_bytes=16 << 20),
        name="own_kernels",
    )(choice, pinned(own), pinned(migration), gain_table)

    turn = (0, 1, 2, 4, 3)
    shifts = coarse_shift.transpose(turn)
    shapes = [jax.ShapeDtypeStruct((n,) + shifts.shape[1:], jnp.float32) for n in (7, 3)]
    scores, displacement = pl.pallas_call(
        track,
        in_specs=[scalars, scalars] + on_chip(10),
        out_specs=on_chip(2),
        out_shape=shapes,
        scratch_shapes=[
            pltpu.VMEM((VOLUME, LANES), jnp.float32),
            pltpu.VMEM((12, GROUPS * SUMS, LANES), jnp.float32),
            pltpu.VMEM((LANES + 16, LANES), jnp.float32),
        ],
        compiler_params=pltpu.CompilerParams(vmem_limit_bytes=24 << 20),
        name="track",
    )(
        choice,
        shifts,
        pinned(kept),
        pinned(received),
        pinned(migration),
        gain_table,
        *[pinned(array) for array in kernel_arrays],
        shifts,
    )
    return scores.transpose(turn), displacement.transpose(turn)


def solution(mesh):
    blocks = P(None, "frame", None, None, "slab")
    placed = (P("slab", "frame", None), P(), P(), P("slab"), blocks, P())
    return jax.shard_map(
        per_device, mesh=mesh, in_specs=placed, out_specs=(blocks, blocks), check_vma=False
    )
```

```python
import functools
import math

import jax
import jax.numpy as jnp
from jax import lax
from jax.experimental import pallas as pl
from jax.experimental.pallas import tpu as pltpu
from jax.sharding import PartitionSpec as P

LX = 32
LY = 64
KX = 8
KY = 8
KZ = 16
CMAX = 8
MARGIN = CMAX + 1
EPSILON = 1e-05

LANES = 128
STEP = 64
EDGE = 16
WINDOW = STEP + 2 * EDGE
SEGMENT = 32
PACKED = STEP // KZ
BX = LX // KX
BY = LY // KY
GROUPS = BX * BY
NX = LX + 2 * MARGIN
NY = 89
KROWS = 145
SPREAD = LX * KROWS + 7
VOLUME = NX * NY + 6
SUMS = 9
CELLS = KX * KY * KZ
STRIP = 4
LATE = False


def pieces_of(value):
    high = value.astype(jnp.bfloat16).astype(jnp.float32)
    middle = (value - high).astype(jnp.bfloat16).astype(jnp.float32)
    return high, middle, value - high - middle


def window_rows(element_data, depth_gain, windows, held, gain, row, arrived):
    columns = element_data.shape[1] // LANES
    copies = [pltpu.make_async_copy(depth_gain, gain, arrived.at[columns])]
    for column in range(columns):
        part = element_data.at[:, column * LANES : (column + 1) * LANES]
        copies.append(pltpu.make_async_copy(part, held.at[column], arrived.at[column]))
    for copy in copies:
        copy.start()
    row[...] = jnp.zeros(row.shape, jnp.float32)
    copies[0].wait()
    for index, piece in enumerate(pieces_of(gain[...])):
        row[index : index + 1, :STEP] = piece
    note = row[...].astype(jnp.bfloat16)
    slabs = windows.shape[0]
    empty = jnp.zeros((EDGE, LANES), jnp.bfloat16)
    spare = lax.broadcasted_iota(jnp.int32, (EDGE, LANES), 0) < 3

    def put(slab, first, rows):
        if 0 <= slab < slabs:
            if first == 0:
                rows = jnp.where(spare, note, rows)
            windows[slab, first : first + EDGE, :] = rows

    put(0, 0, empty)
    put(slabs - 1, EDGE + STEP, empty)
    for column in range(columns):
        copies[1 + column].wait()
        turned = jnp.transpose(held[column])
        for unit in range(LANES // EDGE):
            slab, place = divmod(column * LANES + unit * EDGE, STEP)
            rows = turned[unit * EDGE : (unit + 1) * EDGE]
            put(slab, place + EDGE, rows)
            if place == STEP - EDGE:
                put(slab + 1, 0, rows)
            if place == 0:
                put(slab - 1, EDGE + STEP, rows)


def depth_row(choice, samples):
    lane = lax.broadcasted_iota(jnp.int32, (8, LANES), 1)

    def of(which):
        note = samples[choice[which], :EDGE, :].astype(jnp.float32)
        return jnp.broadcast_to(note[0:1] + note[1:2] + note[2:3], (8, LANES))

    row = pltpu.roll(of(2), EDGE, 1)
    row = jnp.where(lane < EDGE, pltpu.roll(of(1), (EDGE - STEP) % LANES, 1), row)
    return jnp.where(lane >= EDGE + STEP, pltpu.roll(of(3), EDGE + STEP, 1), row)


def migrate(right, migration, columns, gains, store, begin, end):
    raw = lax.dot_general(
        migration[begin * LY : end * LY, :],
        right,
        (((1,), (1,)), ((), ())),
        preferred_element_type=jnp.float32,
    )
    for x in range(begin, end):
        row = x * LY
        gain = columns[row % LANES : row % LANES + LY, row // LANES : row // LANES + 1]
        image = raw[(x - begin) * LY : (x - begin + 1) * LY] * jnp.broadcast_to(gain, (LY, LANES))
        store(x, (image * gains).astype(jnp.bfloat16).astype(jnp.float32))


def own_kernels(
    choice, own, migration, column_gain, kernels, deeper, shallower, edges, powers
):
    gap = jnp.zeros((SEGMENT - KZ, migration.shape[1]), jnp.bfloat16)
    rows = []
    for j in range(PACKED):
        pieces = [own[b, EDGE + j * KZ : EDGE + (j + 1) * KZ, :] for b in range(own.shape[0])]
        rows += [jnp.concatenate(pieces, axis=1), gap]
    lane = lax.broadcasted_iota(jnp.int32, (8, LANES), 1)
    note = own[choice[1], :EDGE, :].astype(jnp.float32)
    row = jnp.broadcast_to(note[0:1] + note[1:2] + note[2:3], (8, LANES))
    gains = row
    for j in range(1, PACKED):
        gains = jnp.where(lane >= j * SEGMENT, pltpu.roll(row, j * KZ, 1), gains)
    for x in range(LX):
        for by in range(BY + 1):
            kernels[x * KROWS + by * 16 : x * KROWS + by * 16 + 8, :] = jnp.zeros((8, LANES))

    def store(x, image):
        for by in range(BY):
            row = x * KROWS + 8 + by * 16
            kernel = image[by * KY : (by + 1) * KY]
            kernels[row : row + 8, :] = kernel
            row = x * LY + by * KY
            shallower[row : row + 8, :] = pltpu.roll(kernel, LANES - 1, 1)
            deeper[row : row + 8, :] = pltpu.roll(kernel, 1, 1)

    right = jnp.concatenate(rows)
    columns = jnp.transpose(column_gain[...])
    for x in range(0, LX, STRIP):
        migrate(right, migration, columns, gains[:1], store, x, x + STRIP)
    for g in range(GROUPS):
        base = g // BY * KX * KROWS + g % BY * 16 + 8
        power = None
        for x in range(KX):
            kernel = kernels[base + x * KROWS : base + x * KROWS + 8, :]
            power = kernel * kernel if power is None else power + kernel * kernel
        powers[g * SUMS : g * SUMS + 8, :] = power
        for index, row in enumerate((base, base + KY - 1)):
            edges[index, g * 8 : g * 8 + 8, :] = kernels[pl.ds(row, 8, stride=KROWS), :]


def track(
    choice,
    shift_table,
    kept,
    received,
    migration,
    column_gain,
    kernels,
    deeper,
    shallower,
    edges,
    kernel_powers,
    shift_cells,
    scores,
    displacement,
    volume,
    sums,
    turned,
    shift,
    arrived,
):
    positions = pltpu.make_async_copy(shift_table, shift, arrived)
    positions.start()
    keep = choice[0] == 1
    zero = jnp.zeros((NY, LANES), jnp.float32)
    for x in list(range(MARGIN)) + list(range(LX + MARGIN, NX)):
        volume[x * NY : (x + 1) * NY, :] = zero
    for x in range(MARGIN, LX + MARGIN):
        volume[x * NY : x * NY + MARGIN, :] = zero[:MARGIN]
        volume[x * NY + MARGIN + LY : (x + 1) * NY, :] = zero[: NY - MARGIN - LY]

    def store(x, image):
        base = (x + MARGIN) * NY + MARGIN
        volume[base : base + LY, :] = image

    pieces = [jnp.where(keep, kept[b], received[b]) for b in range(kept.shape[0])]
    spare = jnp.zeros((LANES - WINDOW, migration.shape[1]), jnp.bfloat16)
    right = jnp.concatenate([jnp.concatenate(pieces, axis=1), spare])
    columns = jnp.transpose(column_gain[...])
    gains = depth_row(choice, kept)[:1]

    def strip(begin, end):
        migrate(right, migration, columns, gains, store, begin, end)

    place = lax.broadcasted_iota(jnp.int32, (16, LANES), 1)
    segment = [((place + 8) & (LANES - 1)) // SEGMENT == j for j in range(PACKED)]
    row_number = lax.broadcasted_iota(jnp.int32, (8, LANES), 0)

    def group(bx, by):
        g = bx * BY + by
        starts = []
        turns = []
        for j in range(PACKED):
            first = bx * KX + MARGIN + shift[0, 0, bx, j, by]
            second = by * KY + MARGIN + shift[1, 0, bx, j, by]
            starts.append(first * NY + second)
            turns.append((j * KZ - EDGE + LANES - shift[2, 0, bx, j, by]) & (LANES - 1))

        def gather(offsets, stride=None):
            value = None
            for j in range(PACKED):
                pair = []
                for offset in offsets:
                    if stride is None:
                        pair.append(volume[pl.ds(starts[j] + offset, 8), :])
                    else:
                        pair.append(volume[pl.ds(starts[j] + offset, 8, stride=stride), :])
                rows = jnp.concatenate(pair).astype(jnp.bfloat16)
                rows = pltpu.roll(rows, turns[j], 1)
                value = rows if value is None else jnp.where(segment[j], rows, value)
            value = value.astype(jnp.float32)
            return [value[:8], value[8:]]

        window = []
        for x in range(-1, KX, 2):
            window += gather((x * NY, (x + 1) * NY))
        before, after = gather((-1, KY), NY)
        square = [value * value for value in window]
        middle = square[2]
        for x in range(3, KX):
            middle = middle + square[x]
        pair_low = square[0] + square[1]
        pair_high = square[KX] + square[KX + 1]
        center = middle + (square[1] + square[KX])
        cross = [None] * 7

        def add(index, value):
            cross[index] = value if cross[index] is None else cross[index] + value

        base = bx * KX * KROWS + by * 16 + 8
        flat = bx * KX * LY + by * KY
        for x in range(KX):
            row = base + x * KROWS
            kernel = kernels[pl.ds(row, 8), :]
            add(0, kernel * window[x + 1])
            add(1, kernel * window[x])
            add(2, kernel * window[x + 2])
            add(3, kernels[pl.ds(row + 1, 8), :] * window[x + 1])
            add(4, kernels[pl.ds(row - 1, 8), :] * window[x + 1])
            aligned = pl.ds(flat + x * LY, 8)
            add(5, shallower[aligned, :] * window[x + 1])
            add(6, deeper[aligned, :] * window[x + 1])
        rows = pl.ds(g * 8, 8)
        add(3, edges[0, rows, :] * before)
        add(4, edges[1, rows, :] * after)
        low = jnp.where(row_number < KY - 1, center, 0.0) + before * before
        high = jnp.where(row_number > 0, center, 0.0) + after * after
        held = cross[:5] + [center, middle + pair_low, middle + pair_high]
        held += [low, high, cross[5], cross[6]]
        for index, value in enumerate(held):
            sums[index, pl.ds(g * SUMS, 8), :] = value

    strips = [(x, min(x + STRIP, LX)) for x in range(0, LX, STRIP)]
    for bx in range(BX):
        reach = min(KX * bx + KX + CMAX, LX - 1) if LATE else LX - 1
        while strips and strips[0][0] <= reach:
            strip(*strips.pop(0))
        if bx == 0:
            positions.wait()
        for by in range(BY):
            group(bx, by)

    def rows_of(index):
        parts = []
        for bx in range(BX):
            value = None
            for y in range(KY):
                place = pl.ds(bx * BY * SUMS + y, BY, stride=SUMS)
                rows = sums[index, place, :] if index < 12 else kernel_powers[place, :]
                value = rows if value is None else value + rows
            parts.append(value)
        return parts

    row_of_block = lax.broadcasted_iota(jnp.int32, (8, LANES), 0)

    def totals(block, offsets):
        value = jnp.transpose(jnp.concatenate([part for index in block for part in rows_of(index)]))
        turned[0:8, :] = value[LANES - 8 :]
        turned[8 : LANES + 8, :] = value
        turned[LANES + 8 : LANES + 16, :] = value[:8]
        result = []
        for offset in offsets:
            total = None
            for j in range(PACKED):
                row = 8 + j * SEGMENT + offset
                value = turned[row : row + 8, :] + turned[row + 8 : row + 16, :]
                value = jnp.broadcast_to(jnp.sum(value, axis=0, keepdims=True), (8, LANES))
                total = value if total is None else jnp.where(row_of_block >= j, value, total)
            result.append(total)
        return result

    def lanes_of(value, place):
        return value if place == 0 else pltpu.roll(value, LANES - place * GROUPS, 1)

    (first,) = totals((0, 1, 2, 3), (0,))
    second, second_low, second_high = totals((4, 5, 6, 7), (0, -1, 1))
    third, third_low, third_high = totals((8, 9, 10, 11), (0, -1, 1))
    (fourth,) = totals((12, 12, 12, 12), (0,))
    cross = [lanes_of(first, place) for place in range(4)]
    cross += [second, lanes_of(third_low, 2), lanes_of(third_high, 3)]
    powers = [lanes_of(second, place) for place in (1, 2, 3)]
    powers += [third, lanes_of(third, 1), lanes_of(second_low, 1), lanes_of(second_high, 1)]
    kernel_power = fourth * (1.0 / CELLS) + EPSILON
    result = []
    for index in range(7):
        mean = cross[index] * (1.0 / CELLS)
        window_power = powers[index] * (1.0 / CELLS) + EPSILON
        result.append(math.sqrt(CELLS) * mean / jnp.sqrt(kernel_power * window_power))
    moves = []
    for axis in range(3):
        lower = result[1 + 2 * axis]
        upper = result[2 + 2 * axis]
        curvature = jnp.maximum(2.0 * result[0] - lower - upper, 1.0)
        moves.append((upper - lower) / (2.0 * curvature))
    for bx in range(BX):
        for index in range(7):
            value = pltpu.roll(result[index], (LANES - bx * BY) % LANES, 1)
            scores[index, 0, bx] = value[:PACKED, :BY]
        for axis in range(3):
            value = pltpu.roll(moves[axis], (LANES - bx * BY) % LANES, 1)
            cells = shift_cells[axis, 0, bx].astype(jnp.float32)
            displacement[axis, 0, bx] = cells + value[:PACKED, :BY]


def on_chip(count):
    return [pl.BlockSpec(memory_space=pltpu.VMEM)] * count


def pinned(array):
    return pltpu.with_memory_space_constraint(array, pltpu.VMEM)


def in_hbm(array):
    return pltpu.with_memory_space_constraint(array, pltpu.HBM)


def per_device(element_data, migration, column_gain, depth_gain, coarse_shift, reference_frame):
    elements_here, frames_here, depth = element_data.shape
    depth_here = depth_gain.shape[0]
    slabs = lax.axis_size("slab")
    frames = lax.axis_size("frame")
    elements = elements_here * slabs
    assert frames_here == 1 and depth_here == STEP
    chosen = reference_frame[0]
    frame = lax.axis_index("frame")
    slab = lax.axis_index("slab")
    own_data = element_data.reshape(elements_here, depth)

    if elements_here == LANES:
        windows = pl.pallas_call(
            window_rows,
            in_specs=[pl.BlockSpec(memory_space=pltpu.HBM)] * 2,
            out_specs=on_chip(1)[0],
            out_shape=jax.ShapeDtypeStruct((slabs, WINDOW, LANES), jnp.bfloat16),
            scratch_shapes=[
                pltpu.VMEM((depth // LANES, LANES, LANES), jnp.bfloat16),
                pltpu.VMEM((1, STEP), jnp.float32),
                pltpu.VMEM((EDGE, LANES), jnp.float32),
                pltpu.SemaphoreType.DMA((depth // LANES + 1,)),
            ],
            compiler_params=pltpu.CompilerParams(vmem_limit_bytes=4 << 20),
            name="window_rows",
        )(in_hbm(own_data), in_hbm(depth_gain.reshape(1, STEP)))
        own = lax.all_to_all(windows, "slab", split_axis=0, concat_axis=0, tiled=True)
        places = [(slab - 1) % slabs, slab, (slab + 1) % slabs]
    else:
        turned = jnp.pad(own_data.T, ((EDGE, EDGE), (0, 0)))
        windows = jnp.stack([turned[i * STEP : i * STEP + WINDOW] for i in range(slabs)])
        own = lax.all_to_all(windows, "slab", split_axis=0, concat_axis=0, tiled=True)
        own = own.transpose(1, 0, 2).reshape(WINDOW, elements // LANES, LANES).transpose(1, 0, 2)
        ring = [(i, (i + 1) % slabs) for i in range(slabs)]
        left = lax.ppermute(depth_gain, "slab", ring)
        right = lax.ppermute(depth_gain, "slab", [(j, i) for i, j in ring])
        high = lambda value: lax.reduce_precision(value, 8, 7)
        for place, value in enumerate((left, depth_gain, right)):
            middle = high(value - high(value))
            note = jnp.stack([high(value), middle, value - high(value) - middle])
            own = own.at[place, :3, :STEP].set(note.astype(jnp.bfloat16))
        places = [0, 1, 2]

    places = [jnp.asarray(place, jnp.int32) for place in places]
    gain_table = column_gain.reshape(-1, LANES)
    scalars = pl.BlockSpec(memory_space=pltpu.SMEM)
    own_shapes = [(SPREAD, LANES), (LX * LY, LANES), (LX * LY, LANES)]
    own_shapes += [(2, GROUPS * 8, LANES), (GROUPS * SUMS, LANES)]
    kernel_arrays = pl.pallas_call(
        own_kernels,
        in_specs=[scalars] + on_chip(3),
        out_specs=on_chip(5),
        out_shape=[pltpu.VMEM(shape, jnp.float32) for shape in own_shapes],
        compiler_params=pltpu.CompilerParams(vmem_limit_bytes=16 << 20),
        name="own_kernels",
    )(jnp.stack(places), pinned(own), pinned(migration), gain_table)

    kept = own
    received = own
    bit = 1
    while bit < frames:
        if bit > 1:
            mine = (chosen ^ frame) & (bit // 2) == 0
            kept = jnp.where(mine, kept, received)
        received = lax.ppermute(kept, "frame", [(i, i ^ bit) for i in range(frames)])
        bit *= 2
    keep = ((chosen ^ frame) & (frames // 2) == 0).astype(jnp.int32)
    choice = jnp.stack([keep] + places)

    turn = (0, 1, 2, 4, 3)
    shifts = coarse_shift.transpose(turn)
    shapes = [jax.ShapeDtypeStruct((n,) + shifts.shape[1:], jnp.float32) for n in (7, 3)]
    scores, displacement = pl.pallas_call(
        track,
        in_specs=[scalars, pl.BlockSpec(memory_space=pltpu.HBM)] + on_chip(10),
        out_specs=on_chip(2),
        out_shape=shapes,
        scratch_shapes=[
            pltpu.VMEM((VOLUME, LANES), jnp.float32),
            pltpu.VMEM((12, GROUPS * SUMS, LANES), jnp.float32),
            pltpu.VMEM((LANES + 16, LANES), jnp.float32),
            pltpu.SMEM(shifts.shape, jnp.int32),
            pltpu.SemaphoreType.DMA,
        ],
        compiler_params=pltpu.CompilerParams(vmem_limit_bytes=24 << 20),
        name="track",
    )(
        choice,
        in_hbm(shifts),
        pinned(kept),
        pinned(received),
        pinned(migration),
        gain_table,
        *[pinned(array) for array in kernel_arrays],
        shifts,
    )
    return scores.transpose(turn), displacement.transpose(turn)


def solution(mesh):
    blocks = P(None, "frame", None, None, "slab")
    placed = (P("slab", "frame", None), P(), P(), P("slab"), blocks, P())
    return jax.shard_map(
        per_device, mesh=mesh, in_specs=placed, out_specs=(blocks, blocks), check_vma=False
    )
```

```python
import functools
import math

import jax
import jax.numpy as jnp
from jax import lax
from jax.experimental import pallas as pl
from jax.experimental.pallas import tpu as pltpu
from jax.sharding import PartitionSpec as P

LX = 32
LY = 64
KX = 8
KY = 8
KZ = 16
CMAX = 8
MARGIN = CMAX + 1
EPSILON = 1e-05

LANES = 128
STEP = 64
EDGE = 16
WINDOW = STEP + 2 * EDGE
SEGMENT = 32
PACKED = STEP // KZ
BX = LX // KX
BY = LY // KY
GROUPS = BX * BY
NX = LX + 2 * MARGIN
NY = 89
KROWS = 145
SPREAD = LX * KROWS + 7
VOLUME = NX * NY + 6
SUMS = 9
CELLS = KX * KY * KZ
STRIP = 4
LATE = False


def pieces_of(value):
    high = value.astype(jnp.bfloat16).astype(jnp.float32)
    middle = (value - high).astype(jnp.bfloat16).astype(jnp.float32)
    return high, middle, value - high - middle


def window_rows(slab_number, element_data, depth_gain, windows, held, gain, row, arrived):
    odd = slab_number[0] & 1
    columns = element_data.shape[1] // LANES
    copies = [pltpu.make_async_copy(depth_gain, gain, arrived.at[columns])]
    for column in range(columns):
        part = element_data.at[:, column * LANES : (column + 1) * LANES]
        copies.append(pltpu.make_async_copy(part, held.at[column], arrived.at[column]))
    for copy in copies:
        copy.start()
    row[...] = jnp.zeros(row.shape, jnp.float32)
    copies[0].wait()
    for index, piece in enumerate(pieces_of(gain[...])):
        row[index : index + 1, :STEP] = piece
    note = row[...].astype(jnp.bfloat16)
    slabs = windows.shape[0] * windows.shape[1]
    empty = jnp.zeros((EDGE, LANES), jnp.bfloat16)
    spare = lax.broadcasted_iota(jnp.int32, (EDGE, LANES), 0) < 3

    def put(slab, first, rows):
        if 0 <= slab < slabs:
            if first == 0:
                rows = jnp.where(spare, note, rows)
            windows[odd ^ (slab & 1), slab // 2, first : first + EDGE, :] = rows

    put(0, 0, empty)
    put(slabs - 1, EDGE + STEP, empty)
    for column in range(columns):
        copies[1 + column].wait()
        turned = jnp.transpose(held[column])
        for unit in range(LANES // EDGE):
            slab, place = divmod(column * LANES + unit * EDGE, STEP)
            rows = turned[unit * EDGE : (unit + 1) * EDGE]
            put(slab, place + EDGE, rows)
            if place == STEP - EDGE:
                put(slab + 1, 0, rows)
            if place == 0:
                put(slab - 1, EDGE + STEP, rows)


def depth_row(choice, samples):
    lane = lax.broadcasted_iota(jnp.int32, (8, LANES), 1)

    def of(which):
        note = samples[choice[which], :EDGE, :].astype(jnp.float32)
        return jnp.broadcast_to(note[0:1] + note[1:2] + note[2:3], (8, LANES))

    row = pltpu.roll(of(2), EDGE, 1)
    row = jnp.where(lane < EDGE, pltpu.roll(of(1), (EDGE - STEP) % LANES, 1), row)
    return jnp.where(lane >= EDGE + STEP, pltpu.roll(of(3), EDGE + STEP, 1), row)


def migrate(right, migration, columns, gains, store, begin, end):
    raw = lax.dot_general(
        migration[begin * LY : end * LY, :],
        right,
        (((1,), (1,)), ((), ())),
        preferred_element_type=jnp.float32,
    )
    for x in range(begin, end):
        row = x * LY
        gain = columns[row % LANES : row % LANES + LY, row // LANES : row // LANES + 1]
        image = raw[(x - begin) * LY : (x - begin + 1) * LY] * jnp.broadcast_to(gain, (LY, LANES))
        store(x, (image * gains).astype(jnp.bfloat16).astype(jnp.float32))


def block_table(shifts, table, spread):
    j = lax.broadcasted_iota(jnp.int32, (PACKED, BY), 0)
    by = lax.broadcasted_iota(jnp.int32, (PACKED, BY), 1)
    spread[...] = jnp.zeros(spread.shape, jnp.float32)
    for bx in range(BX):
        first, second, third = (shifts[axis, 0, bx] for axis in range(3))
        start = (first + (bx * KX + MARGIN)) * NY + second + by * KY + MARGIN
        turn = (j * KZ + (LANES - EDGE) - third) & (LANES - 1)
        for index, value in enumerate((start, turn)):
            row = index * BX * PACKED + bx * PACKED
            spread[row : row + PACKED, :BY] = value.astype(jnp.float32)
    rows = BX * PACKED
    row = lax.broadcasted_iota(jnp.int32, (rows, LANES), 0)
    lane = lax.broadcasted_iota(jnp.int32, (rows, LANES), 1)
    for index in range(2):
        value = spread[index * rows : (index + 1) * rows, :]
        value = pltpu.roll(value, 0, 1, stride=BY, stride_axis=0)
        value = jnp.sum(jnp.where(lane // BY == row, value, 0.0), axis=0, keepdims=True)
        table[index : index + 1, :] = value.astype(jnp.int32)


def own_kernels(
    choice,
    own,
    migration_source,
    column_gain,
    shift_source,
    kernels,
    deeper,
    shallower,
    edges,
    powers,
    table,
    shifts,
    columns,
    migration,
    spread,
    gain_rows,
    arrived,
):
    strips = [(x, x + STRIP) for x in range(0, LX, STRIP)]
    copies = [
        pltpu.make_async_copy(column_gain, gain_rows, arrived.at[len(strips)]),
        pltpu.make_async_copy(shift_source, shifts, arrived.at[len(strips) + 1]),
    ]
    for index, (begin, end) in enumerate(strips):
        rows = pl.ds(begin * LY, (end - begin) * LY)
        copies.append(
            pltpu.make_async_copy(
                migration_source.at[rows, :], migration.at[rows, :], arrived.at[index]
            )
        )
    for copy in copies:
        copy.start()
    gap = jnp.zeros((SEGMENT - KZ, migration.shape[1]), jnp.bfloat16)
    rows = []
    for j in range(PACKED):
        cells = slice(EDGE + j * KZ, EDGE + (j + 1) * KZ)
        pieces = [own[b ^ choice[3], cells, :] for b in range(own.shape[0])]
        rows += [jnp.concatenate(pieces, axis=1), gap]
    lane = lax.broadcasted_iota(jnp.int32, (8, LANES), 1)
    note = own[choice[1], :EDGE, :].astype(jnp.float32)
    row = jnp.broadcast_to(note[0:1] + note[1:2] + note[2:3], (8, LANES))
    gains = row
    for j in range(1, PACKED):
        gains = jnp.where(lane >= j * SEGMENT, pltpu.roll(row, j * KZ, 1), gains)
    for x in range(LX):
        for by in range(BY + 1):
            kernels[x * KROWS + by * 16 : x * KROWS + by * 16 + 8, :] = jnp.zeros((8, LANES))

    def store(x, image):
        for by in range(BY):
            row = x * KROWS + 8 + by * 16
            kernel = image[by * KY : (by + 1) * KY]
            kernels[row : row + 8, :] = kernel
            row = x * LY + by * KY
            shallower[row : row + 8, :] = pltpu.roll(kernel, LANES - 1, 1)
            deeper[row : row + 8, :] = pltpu.roll(kernel, 1, 1)

    right = jnp.concatenate(rows)
    copies[0].wait()
    columns[...] = jnp.transpose(gain_rows[...])
    copies[1].wait()
    block_table(shifts, table, spread)
    for copy, (begin, end) in zip(copies[2:], strips):
        copy.wait()
        migrate(right, migration, columns, gains[:1], store, begin, end)
    for g in range(GROUPS):
        base = g // BY * KX * KROWS + g % BY * 16 + 8
        power = None
        for x in range(KX):
            kernel = kernels[base + x * KROWS : base + x * KROWS + 8, :]
            power = kernel * kernel if power is None else power + kernel * kernel
        powers[g * SUMS : g * SUMS + 8, :] = power
        for index, row in enumerate((base, base + KY - 1)):
            edges[index, g * 8 : g * 8 + 8, :] = kernels[pl.ds(row, 8, stride=KROWS), :]


def track(
    choice,
    kept,
    received,
    kernels,
    deeper,
    shallower,
    edges,
    kernel_powers,
    table,
    shift_cells,
    columns,
    migration,
    scores,
    displacement,
    volume,
    sums,
    turned,
    block,
    arrived,
):
    positions = pltpu.make_async_copy(table, block, arrived)
    positions.start()
    keep = choice[0] == 1
    zero = jnp.zeros((NY, LANES), jnp.float32)
    for x in list(range(MARGIN)) + list(range(LX + MARGIN, NX)):
        volume[x * NY : (x + 1) * NY, :] = zero
    for x in range(MARGIN, LX + MARGIN):
        volume[x * NY : x * NY + MARGIN, :] = zero[:MARGIN]
        volume[x * NY + MARGIN + LY : (x + 1) * NY, :] = zero[: NY - MARGIN - LY]

    def store(x, image):
        base = (x + MARGIN) * NY + MARGIN
        volume[base : base + LY, :] = image

    places = [b ^ choice[4] for b in range(kept.shape[0])]
    pieces = [jnp.where(keep, kept[place], received[place]) for place in places]
    spare = jnp.zeros((LANES - WINDOW, migration.shape[1]), jnp.bfloat16)
    right = jnp.concatenate([jnp.concatenate(pieces, axis=1), spare])
    gains = depth_row(choice, kept)[:1]

    def strip(begin, end):
        migrate(right, migration, columns, gains, store, begin, end)

    place = lax.broadcasted_iota(jnp.int32, (16, LANES), 1)
    segment = [((place + 8) & (LANES - 1)) // SEGMENT == j for j in range(PACKED)]
    row_number = lax.broadcasted_iota(jnp.int32, (8, LANES), 0)

    def group(bx, by):
        g = bx * BY + by
        number = [(bx * PACKED + j) * BY + by for j in range(PACKED)]
        starts = [block[0, n] for n in number]
        turns = [block[1, n] for n in number]

        def gather(offsets, stride=None):
            value = None
            for j in range(PACKED):
                pair = []
                for offset in offsets:
                    if stride is None:
                        pair.append(volume[pl.ds(starts[j] + offset, 8), :])
                    else:
                        pair.append(volume[pl.ds(starts[j] + offset, 8, stride=stride), :])
                rows = jnp.concatenate(pair).astype(jnp.bfloat16)
                rows = pltpu.roll(rows, turns[j], 1)
                value = rows if value is None else jnp.where(segment[j], rows, value)
            value = value.astype(jnp.float32)
            return [value[:8], value[8:]]

        window = []
        for x in range(-1, KX, 2):
            window += gather((x * NY, (x + 1) * NY))
        before, after = gather((-1, KY), NY)
        square = [value * value for value in window]
        middle = square[2]
        for x in range(3, KX):
            middle = middle + square[x]
        pair_low = square[0] + square[1]
        pair_high = square[KX] + square[KX + 1]
        center = middle + (square[1] + square[KX])
        cross = [None] * 7

        def add(index, value):
            cross[index] = value if cross[index] is None else cross[index] + value

        base = bx * KX * KROWS + by * 16 + 8
        flat = bx * KX * LY + by * KY
        for x in range(KX):
            row = base + x * KROWS
            kernel = kernels[pl.ds(row, 8), :]
            add(0, kernel * window[x + 1])
            add(1, kernel * window[x])
            add(2, kernel * window[x + 2])
            add(3, kernels[pl.ds(row + 1, 8), :] * window[x + 1])
            add(4, kernels[pl.ds(row - 1, 8), :] * window[x + 1])
            aligned = pl.ds(flat + x * LY, 8)
            add(5, shallower[aligned, :] * window[x + 1])
            add(6, deeper[aligned, :] * window[x + 1])
        rows = pl.ds(g * 8, 8)
        add(3, edges[0, rows, :] * before)
        add(4, edges[1, rows, :] * after)
        low = jnp.where(row_number < KY - 1, center, 0.0) + before * before
        high = jnp.where(row_number > 0, center, 0.0) + after * after
        held = cross[:5] + [center, middle + pair_low, middle + pair_high]
        held += [low, high, cross[5], cross[6]]
        for index, value in enumerate(held):
            sums[index, pl.ds(g * SUMS, 8), :] = value

    strips = [(x, min(x + STRIP, LX)) for x in range(0, LX, STRIP)]
    for bx in range(BX):
        reach = min(KX * bx + KX + CMAX, LX - 1) if LATE else LX - 1
        while strips and strips[0][0] <= reach:
            strip(*strips.pop(0))
        if bx == 0:
            positions.wait()
        for by in range(BY):
            group(bx, by)

    def rows_of(index):
        parts = []
        for bx in range(BX):
            value = None
            for y in range(KY):
                place = pl.ds(bx * BY * SUMS + y, BY, stride=SUMS)
                rows = sums[index, place, :] if index < 12 else kernel_powers[place, :]
                value = rows if value is None else value + rows
            parts.append(value)
        return parts

    row_of_block = lax.broadcasted_iota(jnp.int32, (8, LANES), 0)

    def totals(block, offsets):
        value = jnp.transpose(jnp.concatenate([part for index in block for part in rows_of(index)]))
        turned[0:8, :] = value[LANES - 8 :]
        turned[8 : LANES + 8, :] = value
        turned[LANES + 8 : LANES + 16, :] = value[:8]
        result = []
        for offset in offsets:
            total = None
            for j in range(PACKED):
                row = 8 + j * SEGMENT + offset
                value = turned[row : row + 8, :] + turned[row + 8 : row + 16, :]
                value = jnp.broadcast_to(jnp.sum(value, axis=0, keepdims=True), (8, LANES))
                total = value if total is None else jnp.where(row_of_block >= j, value, total)
            result.append(total)
        return result

    def lanes_of(value, place):
        return value if place == 0 else pltpu.roll(value, LANES - place * GROUPS, 1)

    (first,) = totals((0, 1, 2, 3), (0,))
    second, second_low, second_high = totals((4, 5, 6, 7), (0, -1, 1))
    third, third_low, third_high = totals((8, 9, 10, 11), (0, -1, 1))
    (fourth,) = totals((12, 12, 12, 12), (0,))
    cross = [lanes_of(first, place) for place in range(4)]
    cross += [second, lanes_of(third_low, 2), lanes_of(third_high, 3)]
    powers = [lanes_of(second, place) for place in (1, 2, 3)]
    powers += [third, lanes_of(third, 1), lanes_of(second_low, 1), lanes_of(second_high, 1)]
    kernel_power = fourth * (1.0 / CELLS) + EPSILON
    result = []
    for index in range(7):
        mean = cross[index] * (1.0 / CELLS)
        window_power = powers[index] * (1.0 / CELLS) + EPSILON
        result.append(math.sqrt(CELLS) * mean / jnp.sqrt(kernel_power * window_power))
    moves = []
    for axis in range(3):
        lower = result[1 + 2 * axis]
        upper = result[2 + 2 * axis]
        curvature = jnp.maximum(2.0 * result[0] - lower - upper, 1.0)
        moves.append((upper - lower) / (2.0 * curvature))
    for bx in range(BX):
        for index in range(7):
            value = pltpu.roll(result[index], (LANES - bx * BY) % LANES, 1)
            scores[index, 0, bx] = value[:PACKED, :BY]
        for axis in range(3):
            value = pltpu.roll(moves[axis], (LANES - bx * BY) % LANES, 1)
            cells = shift_cells[axis, 0, bx].astype(jnp.float32)
            displacement[axis, 0, bx] = cells + value[:PACKED, :BY]


def on_chip(count):
    return [pl.BlockSpec(memory_space=pltpu.VMEM)] * count


def pinned(array):
    return pltpu.with_memory_space_constraint(array, pltpu.VMEM)


def in_hbm(array):
    return pltpu.with_memory_space_constraint(array, pltpu.HBM)


def per_device(element_data, migration, column_gain, depth_gain, coarse_shift, reference_frame):
    elements_here, frames_here, depth = element_data.shape
    depth_here = depth_gain.shape[0]
    slabs = lax.axis_size("slab")
    frames = lax.axis_size("frame")
    elements = elements_here * slabs
    assert frames_here == 1 and depth_here == STEP
    chosen = reference_frame[0]
    frame = lax.axis_index("frame")
    slab = lax.axis_index("slab")
    own_data = element_data.reshape(elements_here, depth)
    scalars = pl.BlockSpec(memory_space=pltpu.SMEM)

    if elements_here == LANES:
        windows = pl.pallas_call(
            window_rows,
            in_specs=[scalars] + [pl.BlockSpec(memory_space=pltpu.HBM)] * 2,
            out_specs=on_chip(1)[0],
            out_shape=jax.ShapeDtypeStruct((2, slabs // 2, WINDOW, LANES), jnp.bfloat16),
            scratch_shapes=[
                pltpu.VMEM((depth // LANES, LANES, LANES), jnp.bfloat16),
                pltpu.VMEM((1, STEP), jnp.float32),
                pltpu.VMEM((EDGE, LANES), jnp.float32),
                pltpu.SemaphoreType.DMA((depth // LANES + 1,)),
            ],
            compiler_params=pltpu.CompilerParams(vmem_limit_bytes=4 << 20),
            name="window_rows",
        )(slab.reshape(1), in_hbm(own_data), in_hbm(depth_gain.reshape(1, STEP)))
        swap = lambda array, bits: lax.ppermute(
            array, "slab", [(i, i ^ bits) for i in range(slabs)]
        )
        halves = (windows[0], swap(windows[1], 1))
        own = []
        for bits in range(slabs // 2):
            pair = jnp.stack(
                [
                    lax.dynamic_index_in_dim(half, slab // 2 ^ bits, 0, keepdims=False)
                    for half in halves
                ]
            )
            own.append(swap(pair, 2 * bits) if bits else pair)
        own = jnp.concatenate(own)
        order = slab
        places = [(slab + step & slabs - 1) ^ slab for step in (-1, 0, 1)]
    else:
        turned = jnp.pad(own_data.T, ((EDGE, EDGE), (0, 0)))
        windows = jnp.stack([turned[i * STEP : i * STEP + WINDOW] for i in range(slabs)])
        own = lax.all_to_all(windows, "slab", split_axis=0, concat_axis=0, tiled=True)
        own = own.transpose(1, 0, 2).reshape(WINDOW, elements // LANES, LANES).transpose(1, 0, 2)
        ring = [(i, (i + 1) % slabs) for i in range(slabs)]
        left = lax.ppermute(depth_gain, "slab", ring)
        right = lax.ppermute(depth_gain, "slab", [(j, i) for i, j in ring])
        high = lambda value: lax.reduce_precision(value, 8, 7)
        for place, value in enumerate((left, depth_gain, right)):
            middle = high(value - high(value))
            note = jnp.stack([high(value), middle, value - high(value) - middle])
            own = own.at[place, :3, :STEP].set(note.astype(jnp.bfloat16))
        order = 0
        places = [0, 1, 2]

    places = [jnp.asarray(place, jnp.int32) for place in places + [order]]
    gain_table = column_gain.reshape(-1, LANES)
    turn = (0, 1, 2, 4, 3)
    shifts = coarse_shift.transpose(turn)
    own_shapes = [(SPREAD, LANES), (LX * LY, LANES), (LX * LY, LANES)]
    own_shapes += [(2, GROUPS * 8, LANES), (GROUPS * SUMS, LANES)]
    kernel_arrays = pl.pallas_call(
        own_kernels,
        in_specs=[scalars] + on_chip(1) + [pl.BlockSpec(memory_space=pltpu.HBM)] * 3,
        out_specs=on_chip(9),
        out_shape=[pltpu.VMEM(shape, jnp.float32) for shape in own_shapes]
        + [
            pltpu.VMEM((8, LANES), jnp.int32),
            pltpu.VMEM(shifts.shape, jnp.int32),
            pltpu.VMEM((LANES, LX * LY // LANES), jnp.float32),
            pltpu.VMEM(migration.shape, jnp.bfloat16),
        ],
        scratch_shapes=[
            pltpu.VMEM((2 * BX * PACKED, LANES), jnp.float32),
            pltpu.VMEM((LX * LY // LANES, LANES), jnp.float32),
            pltpu.SemaphoreType.DMA((LX // STRIP + 2,)),
        ],
        compiler_params=pltpu.CompilerParams(vmem_limit_bytes=16 << 20),
        name="own_kernels",
    )(jnp.stack(places), pinned(own), in_hbm(migration), in_hbm(gain_table), in_hbm(shifts))

    kept = own
    received = own
    bit = 1
    while bit < frames:
        if bit > 1:
            mine = (chosen ^ frame) & (bit // 2) == 0
            kept = jnp.where(mine, kept, received)
        received = lax.ppermute(kept, "frame", [(i, i ^ bit) for i in range(frames)])
        bit *= 2
    keep = ((chosen ^ frame) & (frames // 2) == 0).astype(jnp.int32)
    choice = jnp.stack([keep] + places)

    shapes = [jax.ShapeDtypeStruct((n,) + shifts.shape[1:], jnp.float32) for n in (7, 3)]
    scores, displacement = pl.pallas_call(
        track,
        in_specs=[scalars] + on_chip(11),
        out_specs=on_chip(2),
        out_shape=shapes,
        scratch_shapes=[
            pltpu.VMEM((VOLUME, LANES), jnp.float32),
            pltpu.VMEM((12, GROUPS * SUMS, LANES), jnp.float32),
            pltpu.VMEM((LANES + 16, LANES), jnp.float32),
            pltpu.SMEM((8, LANES), jnp.int32),
            pltpu.SemaphoreType.DMA,
        ],
        compiler_params=pltpu.CompilerParams(vmem_limit_bytes=24 << 20),
        name="track",
    )(
        choice,
        pinned(kept),
        pinned(received),
        *[pinned(array) for array in kernel_arrays],
    )
    return scores.transpose(turn), displacement.transpose(turn)


def solution(mesh):
    blocks = P(None, "frame", None, None, "slab")
    placed = (P("slab", "frame", None), P(), P(), P("slab"), blocks, P())
    return jax.shard_map(
        per_device, mesh=mesh, in_specs=placed, out_specs=(blocks, blocks), check_vma=False
    )
```

```python
import functools
import math

import jax
import jax.numpy as jnp
from jax import lax
from jax.experimental import pallas as pl
from jax.experimental.pallas import tpu as pltpu
from jax.sharding import PartitionSpec as P

LX = 32
LY = 64
KX = 8
KY = 8
KZ = 16
CMAX = 8
MARGIN = CMAX + 1
EPSILON = 1e-05

LANES = 128
STEP = 64
EDGE = 16
WINDOW = STEP + 2 * EDGE
SEGMENT = 32
PACKED = STEP // KZ
BX = LX // KX
BY = LY // KY
GROUPS = BX * BY
NX = LX + 2 * MARGIN
NY = 89
KROWS = 145
SPREAD = LX * KROWS + 7
VOLUME = NX * NY + 6
SUMS = 9
CELLS = KX * KY * KZ
STRIP = 4
LOAD = 16


def pieces_of(value):
    high = value.astype(jnp.bfloat16).astype(jnp.float32)
    middle = (value - high).astype(jnp.bfloat16).astype(jnp.float32)
    return high, middle, value - high - middle


def window_rows(element_data, depth_gain, windows, held, gain, row, arrived):
    columns = element_data.shape[1] // LANES
    copies = [pltpu.make_async_copy(depth_gain, gain, arrived.at[columns])]
    for column in range(columns):
        part = element_data.at[:, column * LANES : (column + 1) * LANES]
        copies.append(pltpu.make_async_copy(part, held.at[column], arrived.at[column]))
    for copy in copies:
        copy.start()
    row[...] = jnp.zeros(row.shape, jnp.float32)
    copies[0].wait()
    for index, piece in enumerate(pieces_of(gain[...])):
        row[index : index + 1, :STEP] = piece
    note = row[...].astype(jnp.bfloat16)
    slabs = windows.shape[0]
    empty = jnp.zeros((EDGE, LANES), jnp.bfloat16)
    spare = lax.broadcasted_iota(jnp.int32, (EDGE, LANES), 0) < 3

    def put(slab, first, rows):
        if 0 <= slab < slabs:
            if first == 0:
                rows = jnp.where(spare, note, rows)
            windows[slab, first : first + EDGE, :] = rows

    put(0, 0, empty)
    put(slabs - 1, EDGE + STEP, empty)
    for column in range(columns):
        copies[1 + column].wait()
        turned = jnp.transpose(held[column])
        for unit in range(LANES // EDGE):
            slab, place = divmod(column * LANES + unit * EDGE, STEP)
            rows = turned[unit * EDGE : (unit + 1) * EDGE]
            put(slab, place + EDGE, rows)
            if place == STEP - EDGE:
                put(slab + 1, 0, rows)
            if place == 0:
                put(slab - 1, EDGE + STEP, rows)


def depth_row(choice, samples):
    lane = lax.broadcasted_iota(jnp.int32, (8, LANES), 1)

    def of(which):
        note = samples[choice[which], :EDGE, :].astype(jnp.float32)
        return jnp.broadcast_to(note[0:1] + note[1:2] + note[2:3], (8, LANES))

    row = pltpu.roll(of(2), EDGE, 1)
    row = jnp.where(lane < EDGE, pltpu.roll(of(1), (EDGE - STEP) % LANES, 1), row)
    return jnp.where(lane >= EDGE + STEP, pltpu.roll(of(3), EDGE + STEP, 1), row)


def migrate(right, migration, columns, gains, store, begin, end):
    raw = lax.dot_general(
        migration[begin * LY : end * LY, :],
        right,
        (((1,), (1,)), ((), ())),
        preferred_element_type=jnp.float32,
    )
    for x in range(begin, end):
        row = x * LY
        gain = columns[row % LANES : row % LANES + LY, row // LANES : row // LANES + 1]
        image = raw[(x - begin) * LY : (x - begin + 1) * LY]
        image = image * jnp.broadcast_to(gain, image.shape)
        store(x, (image * gains).astype(jnp.bfloat16).astype(jnp.float32))


def block_table(shifts, table, spread):
    j = lax.broadcasted_iota(jnp.int32, (PACKED, BY), 0)
    by = lax.broadcasted_iota(jnp.int32, (PACKED, BY), 1)
    spread[...] = jnp.zeros(spread.shape, jnp.float32)
    for bx in range(BX):
        first, second, third = (shifts[axis, 0, bx] for axis in range(3))
        start = (first + (bx * KX + MARGIN)) * NY + second + by * KY + MARGIN
        turn = (j * KZ + (LANES - EDGE) - third) & (LANES - 1)
        for index, value in enumerate((start, turn)):
            row = index * BX * PACKED + bx * PACKED
            spread[row : row + PACKED, :BY] = value.astype(jnp.float32)
    rows = BX * PACKED
    row = lax.broadcasted_iota(jnp.int32, (rows, LANES), 0)
    lane = lax.broadcasted_iota(jnp.int32, (rows, LANES), 1)
    for index in range(2):
        value = spread[index * rows : (index + 1) * rows, :]
        value = pltpu.roll(value, 0, 1, stride=BY, stride_axis=0)
        value = jnp.sum(jnp.where(lane // BY == row, value, 0.0), axis=0, keepdims=True)
        table[index : index + 1, :] = value.astype(jnp.int32)


def own_kernels(
    choice,
    own,
    migration_source,
    column_gain,
    shift_source,
    kernels,
    deeper,
    shallower,
    edges,
    powers,
    table,
    shifts,
    columns,
    migration,
    spread,
    gain_rows,
    arrived,
):
    strips = [(x, x + LOAD) for x in range(0, LX, LOAD)]
    copies = [
        pltpu.make_async_copy(column_gain, gain_rows, arrived.at[len(strips)]),
        pltpu.make_async_copy(shift_source, shifts, arrived.at[len(strips) + 1]),
    ]
    for index, (begin, end) in enumerate(strips):
        rows = pl.ds(begin * LY, (end - begin) * LY)
        copies.append(
            pltpu.make_async_copy(
                migration_source.at[rows, :], migration.at[rows, :], arrived.at[index]
            )
        )
    for copy in copies:
        copy.start()
    gap = jnp.zeros((SEGMENT - KZ, migration.shape[1]), jnp.bfloat16)
    rows = []
    for j in range(PACKED):
        cells = slice(EDGE + j * KZ, EDGE + (j + 1) * KZ)
        pieces = [own[b, cells, :] for b in range(own.shape[0])]
        rows += [jnp.concatenate(pieces, axis=1), gap]
    lane = lax.broadcasted_iota(jnp.int32, (8, LANES), 1)
    note = own[choice[1], :EDGE, :].astype(jnp.float32)
    row = jnp.broadcast_to(note[0:1] + note[1:2] + note[2:3], (8, LANES))
    gains = row
    for j in range(1, PACKED):
        gains = jnp.where(lane >= j * SEGMENT, pltpu.roll(row, j * KZ, 1), gains)
    for x in range(LX):
        for by in range(BY + 1):
            kernels[x * KROWS + by * 16 : x * KROWS + by * 16 + 8, :] = jnp.zeros((8, LANES))

    def store(x, image):
        for by in range(BY):
            row = x * KROWS + 8 + by * 16
            kernel = image[by * KY : (by + 1) * KY]
            kernels[row : row + 8, :] = kernel
            row = x * LY + by * KY
            shallower[row : row + 8, :] = pltpu.roll(kernel, LANES - 1, 1)
            deeper[row : row + 8, :] = pltpu.roll(kernel, 1, 1)

    right = jnp.concatenate(rows)
    copies[0].wait()
    columns[...] = jnp.transpose(gain_rows[...])
    copies[1].wait()
    block_table(shifts, table, spread)
    for copy, (begin, end) in zip(copies[2:], strips):
        copy.wait()
        migrate(right, migration, columns, gains[:1], store, begin, end)
    for g in range(GROUPS):
        base = g // BY * KX * KROWS + g % BY * 16 + 8
        power = None
        for x in range(KX):
            kernel = kernels[base + x * KROWS : base + x * KROWS + 8, :]
            power = kernel * kernel if power is None else power + kernel * kernel
        powers[g * SUMS : g * SUMS + 8, :] = power
        for index, row in enumerate((base, base + KY - 1)):
            edges[index, g * 8 : g * 8 + 8, :] = kernels[pl.ds(row, 8, stride=KROWS), :]


def track(
    choice,
    kept,
    received,
    kernels,
    deeper,
    shallower,
    edges,
    kernel_powers,
    table,
    shift_cells,
    columns,
    migration,
    scores,
    displacement,
    volume,
    sums,
    turned,
    block,
    arrived,
):
    positions = pltpu.make_async_copy(table, block, arrived)
    positions.start()
    keep = choice[0] == 1
    zero = jnp.zeros((NY, LANES), jnp.float32)
    for x in list(range(MARGIN)) + list(range(LX + MARGIN, NX)):
        volume[x * NY : (x + 1) * NY, :] = zero
    for x in range(MARGIN, LX + MARGIN):
        volume[x * NY : x * NY + MARGIN, :] = zero[:MARGIN]
        volume[x * NY + MARGIN + LY : (x + 1) * NY, :] = zero[: NY - MARGIN - LY]

    def store(x, image):
        base = (x + MARGIN) * NY + MARGIN
        volume[base : base + LY, :] = image

    pieces = [jnp.where(keep, kept[b], received[b]) for b in range(kept.shape[0])]
    spare = jnp.zeros((LANES - WINDOW, migration.shape[1]), jnp.bfloat16)
    right = jnp.concatenate([jnp.concatenate(pieces, axis=1), spare])
    gains = depth_row(choice, kept)[:1]

    lane = lax.broadcasted_iota(jnp.int32, (16, LANES), 1)
    segment = [((lane + 8) & (LANES - 1)) // SEGMENT == j for j in range(PACKED)]
    row_number = lax.broadcasted_iota(jnp.int32, (8, LANES), 0)

    def group(bx, by):
        g = bx * BY + by
        number = [(bx * PACKED + j) * BY + by for j in range(PACKED)]
        starts = [block[0, n] for n in number]
        turns = [block[1, n] for n in number]

        def gather(offsets, stride=None):
            value = None
            for j in range(PACKED):
                pair = []
                for offset in offsets:
                    if stride is None:
                        pair.append(volume[pl.ds(starts[j] + offset, 8), :])
                    else:
                        pair.append(volume[pl.ds(starts[j] + offset, 8, stride=stride), :])
                rows = jnp.concatenate(pair).astype(jnp.bfloat16)
                rows = pltpu.roll(rows, turns[j], 1)
                value = rows if value is None else jnp.where(segment[j], rows, value)
            value = value.astype(jnp.float32)
            return [value[:8], value[8:]]

        window = []
        for x in range(-1, KX, 2):
            window += gather((x * NY, (x + 1) * NY))
        before, after = gather((-1, KY), NY)
        square = [value * value for value in window]
        middle = square[2]
        for x in range(3, KX):
            middle = middle + square[x]
        pair_low = square[0] + square[1]
        pair_high = square[KX] + square[KX + 1]
        center = middle + (square[1] + square[KX])
        cross = [None] * 7

        def add(index, value):
            cross[index] = value if cross[index] is None else cross[index] + value

        base = bx * KX * KROWS + by * 16 + 8
        flat = bx * KX * LY + by * KY
        for x in range(KX):
            row = base + x * KROWS
            kernel = kernels[pl.ds(row, 8), :]
            add(0, kernel * window[x + 1])
            add(1, kernel * window[x])
            add(2, kernel * window[x + 2])
            add(3, kernels[pl.ds(row + 1, 8), :] * window[x + 1])
            add(4, kernels[pl.ds(row - 1, 8), :] * window[x + 1])
            aligned = pl.ds(flat + x * LY, 8)
            add(5, shallower[aligned, :] * window[x + 1])
            add(6, deeper[aligned, :] * window[x + 1])
        rows = pl.ds(g * 8, 8)
        add(3, edges[0, rows, :] * before)
        add(4, edges[1, rows, :] * after)
        low = jnp.where(row_number < KY - 1, center, 0.0) + before * before
        high = jnp.where(row_number > 0, center, 0.0) + after * after
        held = cross[:5] + [center, middle + pair_low, middle + pair_high]
        held += [low, high, cross[5], cross[6]]
        for index, value in enumerate(held):
            sums[index, pl.ds(g * SUMS, 8), :] = value

    for x in range(0, LX, STRIP):
        migrate(right, migration, columns, gains, store, x, x + STRIP)
    positions.wait()
    for bx in range(BX):
        for by in range(BY):
            group(bx, by)

    def rows_of(index):
        parts = []
        for bx in range(BX):
            value = None
            for y in range(KY):
                place = pl.ds(bx * BY * SUMS + y, BY, stride=SUMS)
                rows = sums[index, place, :] if index < 12 else kernel_powers[place, :]
                value = rows if value is None else value + rows
            parts.append(value)
        return parts

    row_of_block = lax.broadcasted_iota(jnp.int32, (8, LANES), 0)

    def totals(block, offsets):
        value = jnp.transpose(jnp.concatenate([part for index in block for part in rows_of(index)]))
        turned[0:8, :] = value[LANES - 8 :]
        turned[8 : LANES + 8, :] = value
        turned[LANES + 8 : LANES + 16, :] = value[:8]
        result = []
        for offset in offsets:
            total = None
            for j in range(PACKED):
                row = 8 + j * SEGMENT + offset
                value = turned[row : row + 8, :] + turned[row + 8 : row + 16, :]
                value = jnp.broadcast_to(jnp.sum(value, axis=0, keepdims=True), (8, LANES))
                total = value if total is None else jnp.where(row_of_block >= j, value, total)
            result.append(total)
        return result

    def lanes_of(value, place):
        return value if place == 0 else pltpu.roll(value, LANES - place * GROUPS, 1)

    (first,) = totals((0, 1, 2, 3), (0,))
    second, second_low, second_high = totals((4, 5, 6, 7), (0, -1, 1))
    third, third_low, third_high = totals((8, 9, 10, 11), (0, -1, 1))
    (fourth,) = totals((12, 12, 12, 12), (0,))
    cross = [lanes_of(first, place) for place in range(4)]
    cross += [second, lanes_of(third_low, 2), lanes_of(third_high, 3)]
    powers = [lanes_of(second, place) for place in (1, 2, 3)]
    powers += [third, lanes_of(third, 1), lanes_of(second_low, 1), lanes_of(second_high, 1)]
    kernel_power = fourth * (1.0 / CELLS) + EPSILON
    result = []
    for index in range(7):
        mean = cross[index] * (1.0 / CELLS)
        window_power = powers[index] * (1.0 / CELLS) + EPSILON
        result.append(math.sqrt(CELLS) * mean / jnp.sqrt(kernel_power * window_power))
    moves = []
    for axis in range(3):
        lower = result[1 + 2 * axis]
        upper = result[2 + 2 * axis]
        curvature = jnp.maximum(2.0 * result[0] - lower - upper, 1.0)
        moves.append((upper - lower) / (2.0 * curvature))
    for bx in range(BX):
        for index in range(7):
            value = pltpu.roll(result[index], (LANES - bx * BY) % LANES, 1)
            scores[index, 0, bx] = value[:PACKED, :BY]
        for axis in range(3):
            value = pltpu.roll(moves[axis], (LANES - bx * BY) % LANES, 1)
            cells = shift_cells[axis, 0, bx].astype(jnp.float32)
            displacement[axis, 0, bx] = cells + value[:PACKED, :BY]


def on_chip(count):
    return [pl.BlockSpec(memory_space=pltpu.VMEM)] * count


def pinned(array):
    return pltpu.with_memory_space_constraint(array, pltpu.VMEM)


def in_hbm(array):
    return pltpu.with_memory_space_constraint(array, pltpu.HBM)


def per_device(element_data, migration, column_gain, depth_gain, coarse_shift, reference_frame):
    elements_here, frames_here, depth = element_data.shape
    depth_here = depth_gain.shape[0]
    slabs = lax.axis_size("slab")
    frames = lax.axis_size("frame")
    elements = elements_here * slabs
    assert frames_here == 1 and depth_here == STEP
    chosen = reference_frame[0]
    frame = lax.axis_index("frame")
    slab = lax.axis_index("slab")
    own_data = element_data.reshape(elements_here, depth)
    scalars = pl.BlockSpec(memory_space=pltpu.SMEM)

    if elements_here == LANES:
        windows = pl.pallas_call(
            window_rows,
            in_specs=[pl.BlockSpec(memory_space=pltpu.HBM)] * 2,
            out_specs=on_chip(1)[0],
            out_shape=jax.ShapeDtypeStruct((slabs, WINDOW, LANES), jnp.bfloat16),
            scratch_shapes=[
                pltpu.VMEM((depth // LANES, LANES, LANES), jnp.bfloat16),
                pltpu.VMEM((1, STEP), jnp.float32),
                pltpu.VMEM((EDGE, LANES), jnp.float32),
                pltpu.SemaphoreType.DMA((depth // LANES + 1,)),
            ],
            compiler_params=pltpu.CompilerParams(vmem_limit_bytes=4 << 20),
            name="window_rows",
        )(in_hbm(own_data), in_hbm(depth_gain.reshape(1, STEP)))
        own = lax.all_to_all(windows, "slab", split_axis=0, concat_axis=0, tiled=True)
        places = [slab + step & slabs - 1 for step in (-1, 0, 1)]
    else:
        turned = jnp.pad(own_data.T, ((EDGE, EDGE), (0, 0)))
        windows = jnp.stack([turned[i * STEP : i * STEP + WINDOW] for i in range(slabs)])
        own = lax.all_to_all(windows, "slab", split_axis=0, concat_axis=0, tiled=True)
        own = own.transpose(1, 0, 2).reshape(WINDOW, elements // LANES, LANES).transpose(1, 0, 2)
        ring = [(i, (i + 1) % slabs) for i in range(slabs)]
        left = lax.ppermute(depth_gain, "slab", ring)
        right = lax.ppermute(depth_gain, "slab", [(j, i) for i, j in ring])
        high = lambda value: lax.reduce_precision(value, 8, 7)
        for place, value in enumerate((left, depth_gain, right)):
            middle = high(value - high(value))
            note = jnp.stack([high(value), middle, value - high(value) - middle])
            own = own.at[place, :3, :STEP].set(note.astype(jnp.bfloat16))
        places = [0, 1, 2]

    places = [jnp.asarray(place, jnp.int32) for place in places]
    gain_table = column_gain.reshape(-1, LANES)
    turn = (0, 1, 2, 4, 3)
    shifts = coarse_shift.transpose(turn)
    own_shapes = [(SPREAD, LANES), (LX * LY, LANES), (LX * LY, LANES)]
    own_shapes += [(2, GROUPS * 8, LANES), (GROUPS * SUMS, LANES)]
    kernel_arrays = pl.pallas_call(
        own_kernels,
        in_specs=[scalars] + on_chip(1) + [pl.BlockSpec(memory_space=pltpu.HBM)] * 3,
        out_specs=on_chip(9),
        out_shape=[pltpu.VMEM(shape, jnp.float32) for shape in own_shapes]
        + [
            pltpu.VMEM((8, LANES), jnp.int32),
            pltpu.VMEM(shifts.shape, jnp.int32),
            pltpu.VMEM((LANES, LX * LY // LANES), jnp.float32),
            pltpu.VMEM(migration.shape, jnp.bfloat16),
        ],
        scratch_shapes=[
            pltpu.VMEM((2 * BX * PACKED, LANES), jnp.float32),
            pltpu.VMEM((LX * LY // LANES, LANES), jnp.float32),
            pltpu.SemaphoreType.DMA((LX // LOAD + 2,)),
        ],
        compiler_params=pltpu.CompilerParams(vmem_limit_bytes=16 << 20),
        name="own_kernels",
    )(jnp.stack(places), pinned(own), in_hbm(migration), in_hbm(gain_table), in_hbm(shifts))

    kept = own
    received = own
    bit = 1
    while bit < frames:
        if bit > 1:
            mine = (chosen ^ frame) & (bit // 2) == 0
            kept = jnp.where(mine, kept, received)
        received = lax.ppermute(kept, "frame", [(i, i ^ bit) for i in range(frames)])
        bit *= 2
    keep = ((chosen ^ frame) & (frames // 2) == 0).astype(jnp.int32)
    choice = jnp.stack([keep] + places)

    shapes = [jax.ShapeDtypeStruct((n,) + shifts.shape[1:], jnp.float32) for n in (7, 3)]
    scores, displacement = pl.pallas_call(
        track,
        in_specs=[scalars] + on_chip(11),
        out_specs=on_chip(2),
        out_shape=shapes,
        scratch_shapes=[
            pltpu.VMEM((VOLUME, LANES), jnp.float32),
            pltpu.VMEM((12, GROUPS * SUMS, LANES), jnp.float32),
            pltpu.VMEM((LANES + 16, LANES), jnp.float32),
            pltpu.SMEM((8, LANES), jnp.int32),
            pltpu.SemaphoreType.DMA,
        ],
        compiler_params=pltpu.CompilerParams(vmem_limit_bytes=24 << 20),
        name="track",
    )(
        choice,
        pinned(kept),
        pinned(received),
        *[pinned(array) for array in kernel_arrays],
    )
    return scores.transpose(turn), displacement.transpose(turn)


def solution(mesh):
    blocks = P(None, "frame", None, None, "slab")
    placed = (P("slab", "frame", None), P(), P(), P("slab"), blocks, P())
    return jax.shard_map(
        per_device, mesh=mesh, in_specs=placed, out_specs=(blocks, blocks), check_vma=False
    )
```

```python
import functools
import math

import jax
import jax.numpy as jnp
from jax import lax
from jax.experimental import pallas as pl
from jax.experimental.pallas import tpu as pltpu
from jax.sharding import PartitionSpec as P

LX = 32
LY = 64
KX = 8
KY = 8
KZ = 16
CMAX = 8
MARGIN = CMAX + 1
EPSILON = 1e-05

LANES = 128
STEP = 64
EDGE = 16
WINDOW = STEP + 2 * EDGE
SEGMENT = 32
PACKED = STEP // KZ
BX = LX // KX
BY = LY // KY
GROUPS = BX * BY
NX = LX + 2 * MARGIN
NY = 89
KROWS = 145
SPREAD = LX * KROWS + 7
VOLUME = NX * NY + 6
SUMS = 9
CELLS = KX * KY * KZ
STRIP = 4
LOAD = 16


def pieces_of(value):
    high = value.astype(jnp.bfloat16).astype(jnp.float32)
    middle = (value - high).astype(jnp.bfloat16).astype(jnp.float32)
    return high, middle, value - high - middle


def window_rows(element_data, depth_gain, windows, held, gain, row, arrived):
    columns = element_data.shape[1] // LANES
    copies = [pltpu.make_async_copy(depth_gain, gain, arrived.at[columns])]
    for column in range(columns):
        part = element_data.at[:, column * LANES : (column + 1) * LANES]
        copies.append(pltpu.make_async_copy(part, held.at[column], arrived.at[column]))
    for copy in copies:
        copy.start()
    row[...] = jnp.zeros(row.shape, jnp.float32)
    copies[0].wait()
    for index, piece in enumerate(pieces_of(gain[...])):
        row[index : index + 1, :STEP] = piece
    note = row[...].astype(jnp.bfloat16)
    slabs = windows.shape[0]
    empty = jnp.zeros((EDGE, LANES), jnp.bfloat16)
    spare = lax.broadcasted_iota(jnp.int32, (EDGE, LANES), 0) < 3

    def put(slab, first, rows):
        if 0 <= slab < slabs:
            if first == 0:
                rows = jnp.where(spare, note, rows)
            windows[slab, first : first + EDGE, :] = rows

    put(0, 0, empty)
    put(slabs - 1, EDGE + STEP, empty)
    for column in range(columns):
        copies[1 + column].wait()
        turned = jnp.transpose(held[column])
        for unit in range(LANES // EDGE):
            slab, place = divmod(column * LANES + unit * EDGE, STEP)
            rows = turned[unit * EDGE : (unit + 1) * EDGE]
            put(slab, place + EDGE, rows)
            if place == STEP - EDGE:
                put(slab + 1, 0, rows)
            if place == 0:
                put(slab - 1, EDGE + STEP, rows)


def depth_row(choice, samples):
    lane = lax.broadcasted_iota(jnp.int32, (8, LANES), 1)

    def of(which):
        note = samples[choice[which], :EDGE, :].astype(jnp.float32)
        return jnp.broadcast_to(note[0:1] + note[1:2] + note[2:3], (8, LANES))

    row = pltpu.roll(of(2), EDGE, 1)
    row = jnp.where(lane < EDGE, pltpu.roll(of(1), (EDGE - STEP) % LANES, 1), row)
    return jnp.where(lane >= EDGE + STEP, pltpu.roll(of(3), EDGE + STEP, 1), row)


def migrated(right, migration, begin, end, first=0):
    return lax.dot_general(
        migration[begin * LY : end * LY, first : first + right.shape[1]],
        right,
        (((1,), (1,)), ((), ())),
        preferred_element_type=jnp.float32,
    )


def finish(raw, columns, gains, store, begin, end):
    for x in range(begin, end):
        row = x * LY
        gain = columns[row % LANES : row % LANES + LY, row // LANES : row // LANES + 1]
        image = raw[(x - begin) * LY : (x - begin + 1) * LY]
        image = image * jnp.broadcast_to(gain, image.shape)
        store(x, (image * gains).astype(jnp.bfloat16).astype(jnp.float32))


def block_table(shifts, table, spread):
    j = lax.broadcasted_iota(jnp.int32, (PACKED, BY), 0)
    by = lax.broadcasted_iota(jnp.int32, (PACKED, BY), 1)
    spread[...] = jnp.zeros(spread.shape, jnp.float32)
    for bx in range(BX):
        first, second, third = (shifts[axis, 0, bx] for axis in range(3))
        start = (first + (bx * KX + MARGIN)) * NY + second + by * KY + MARGIN
        turn = (j * KZ + (LANES - EDGE) - third) & (LANES - 1)
        for index, value in enumerate((start, turn)):
            row = index * BX * PACKED + bx * PACKED
            spread[row : row + PACKED, :BY] = value.astype(jnp.float32)
    rows = BX * PACKED
    row = lax.broadcasted_iota(jnp.int32, (rows, LANES), 0)
    lane = lax.broadcasted_iota(jnp.int32, (rows, LANES), 1)
    for index in range(2):
        value = spread[index * rows : (index + 1) * rows, :]
        value = pltpu.roll(value, 0, 1, stride=BY, stride_axis=0)
        value = jnp.sum(jnp.where(lane // BY == row, value, 0.0), axis=0, keepdims=True)
        table[index : index + 1, :] = value.astype(jnp.int32)


def own_kernels(
    choice,
    own,
    migration_source,
    column_gain,
    shift_source,
    kernels,
    deeper,
    shallower,
    edges,
    powers,
    table,
    shifts,
    columns,
    migration,
    spread,
    gain_rows,
    arrived,
):
    strips = [(x, x + LOAD) for x in range(0, LX, LOAD)]
    copies = [
        pltpu.make_async_copy(column_gain, gain_rows, arrived.at[len(strips)]),
        pltpu.make_async_copy(shift_source, shifts, arrived.at[len(strips) + 1]),
    ]
    for index, (begin, end) in enumerate(strips):
        rows = pl.ds(begin * LY, (end - begin) * LY)
        copies.append(
            pltpu.make_async_copy(
                migration_source.at[rows, :], migration.at[rows, :], arrived.at[index]
            )
        )
    for copy in copies:
        copy.start()
    gap = jnp.zeros((SEGMENT - KZ, migration.shape[1]), jnp.bfloat16)
    rows = []
    for j in range(PACKED):
        cells = slice(EDGE + j * KZ, EDGE + (j + 1) * KZ)
        pieces = [own[b, cells, :] for b in range(own.shape[0])]
        rows += [jnp.concatenate(pieces, axis=1), gap]
    lane = lax.broadcasted_iota(jnp.int32, (8, LANES), 1)
    note = own[choice[1], :EDGE, :].astype(jnp.float32)
    row = jnp.broadcast_to(note[0:1] + note[1:2] + note[2:3], (8, LANES))
    gains = row
    for j in range(1, PACKED):
        gains = jnp.where(lane >= j * SEGMENT, pltpu.roll(row, j * KZ, 1), gains)
    for x in range(LX):
        for by in range(BY + 1):
            kernels[x * KROWS + by * 16 : x * KROWS + by * 16 + 8, :] = jnp.zeros((8, LANES))

    def store(x, image):
        for by in range(BY):
            row = x * KROWS + 8 + by * 16
            kernel = image[by * KY : (by + 1) * KY]
            kernels[row : row + 8, :] = kernel
            row = x * LY + by * KY
            shallower[row : row + 8, :] = pltpu.roll(kernel, LANES - 1, 1)
            deeper[row : row + 8, :] = pltpu.roll(kernel, 1, 1)

    right = jnp.concatenate(rows)
    copies[0].wait()
    columns[...] = jnp.transpose(gain_rows[...])
    copies[1].wait()
    block_table(shifts, table, spread)
    for copy, (begin, end) in zip(copies[2:], strips):
        copy.wait()
        raw = migrated(right, migration, begin, end)
        finish(raw, columns, gains[:1], store, begin, end)
    for g in range(GROUPS):
        base = g // BY * KX * KROWS + g % BY * 16 + 8
        power = None
        for x in range(KX):
            kernel = kernels[base + x * KROWS : base + x * KROWS + 8, :]
            power = kernel * kernel if power is None else power + kernel * kernel
        powers[g * SUMS : g * SUMS + 8, :] = power
        for index, row in enumerate((base, base + KY - 1)):
            edges[index, g * 8 : g * 8 + 8, :] = kernels[pl.ds(row, 8, stride=KROWS), :]


def reference_samples(choice, kept, received, first):
    keep = choice[0] == 1
    blocks = received.shape[0]
    pieces = [jnp.where(keep, kept[first + b], received[b]) for b in range(blocks)]
    spare = jnp.zeros((LANES - WINDOW, blocks * LANES), jnp.bfloat16)
    return jnp.concatenate([jnp.concatenate(pieces, axis=1), spare])


def reference_part(choice, kept, received, migration, partial):
    right = reference_samples(choice, kept, received, 0)
    for x in range(0, LX, STRIP):
        partial[x * LY : (x + STRIP) * LY, :] = migrated(right, migration, x, x + STRIP)


def track(
    choice,
    kept,
    received,
    partial,
    kernels,
    deeper,
    shallower,
    edges,
    kernel_powers,
    table,
    shift_cells,
    columns,
    migration,
    scores,
    displacement,
    volume,
    sums,
    turned,
    block,
    arrived,
):
    positions = pltpu.make_async_copy(table, block, arrived)
    positions.start()

    def store(x, image):
        base = (x + MARGIN) * NY + MARGIN
        volume[base : base + LY, :] = image

    first = kept.shape[0] - received.shape[0]
    right = reference_samples(choice, kept, received, first)
    gains = depth_row(choice, kept)[:1]
    for x in range(0, LX, STRIP):
        raw = partial[x * LY : (x + STRIP) * LY, :]
        raw = raw + migrated(right, migration, x, x + STRIP, first * LANES)
        finish(raw, columns, gains, store, x, x + STRIP)
    zero = jnp.zeros((NY, LANES), jnp.float32)
    for x in list(range(MARGIN)) + list(range(LX + MARGIN, NX)):
        volume[x * NY : (x + 1) * NY, :] = zero
    for x in range(MARGIN, LX + MARGIN):
        volume[x * NY : x * NY + MARGIN, :] = zero[:MARGIN]
        volume[x * NY + MARGIN + LY : (x + 1) * NY, :] = zero[: NY - MARGIN - LY]
    positions.wait()

    lane = lax.broadcasted_iota(jnp.int32, (16, LANES), 1)
    segment = [((lane + 8) & (LANES - 1)) // SEGMENT == j for j in range(PACKED)]
    row_number = lax.broadcasted_iota(jnp.int32, (8, LANES), 0)

    def group(bx, by):
        g = bx * BY + by
        number = [(bx * PACKED + j) * BY + by for j in range(PACKED)]
        starts = [block[0, n] for n in number]
        turns = [block[1, n] for n in number]

        def gather(offsets, stride=None):
            value = None
            for j in range(PACKED):
                pair = []
                for offset in offsets:
                    if stride is None:
                        pair.append(volume[pl.ds(starts[j] + offset, 8), :])
                    else:
                        pair.append(volume[pl.ds(starts[j] + offset, 8, stride=stride), :])
                rows = jnp.concatenate(pair).astype(jnp.bfloat16)
                rows = pltpu.roll(rows, turns[j], 1)
                value = rows if value is None else jnp.where(segment[j], rows, value)
            value = value.astype(jnp.float32)
            return [value[:8], value[8:]]

        window = []
        for x in range(-1, KX, 2):
            window += gather((x * NY, (x + 1) * NY))
        before, after = gather((-1, KY), NY)
        square = [value * value for value in window]
        middle = square[2]
        for x in range(3, KX):
            middle = middle + square[x]
        pair_low = square[0] + square[1]
        pair_high = square[KX] + square[KX + 1]
        center = middle + (square[1] + square[KX])
        cross = [None] * 7

        def add(index, value):
            cross[index] = value if cross[index] is None else cross[index] + value

        base = bx * KX * KROWS + by * 16 + 8
        flat = bx * KX * LY + by * KY
        for x in range(KX):
            row = base + x * KROWS
            kernel = kernels[pl.ds(row, 8), :]
            add(0, kernel * window[x + 1])
            add(1, kernel * window[x])
            add(2, kernel * window[x + 2])
            add(3, kernels[pl.ds(row + 1, 8), :] * window[x + 1])
            add(4, kernels[pl.ds(row - 1, 8), :] * window[x + 1])
            aligned = pl.ds(flat + x * LY, 8)
            add(5, shallower[aligned, :] * window[x + 1])
            add(6, deeper[aligned, :] * window[x + 1])
        rows = pl.ds(g * 8, 8)
        add(3, edges[0, rows, :] * before)
        add(4, edges[1, rows, :] * after)
        low = jnp.where(row_number < KY - 1, center, 0.0) + before * before
        high = jnp.where(row_number > 0, center, 0.0) + after * after
        held = cross[:5] + [center, middle + pair_low, middle + pair_high]
        held += [low, high, cross[5], cross[6]]
        for index, value in enumerate(held):
            sums[index, pl.ds(g * SUMS, 8), :] = value

    for bx in range(BX):
        for by in range(BY):
            group(bx, by)

    def rows_of(index):
        parts = []
        for bx in range(BX):
            value = None
            for y in range(KY):
                place = pl.ds(bx * BY * SUMS + y, BY, stride=SUMS)
                rows = sums[index, place, :] if index < 12 else kernel_powers[place, :]
                value = rows if value is None else value + rows
            parts.append(value)
        return parts

    row_of_block = lax.broadcasted_iota(jnp.int32, (8, LANES), 0)

    def totals(block, offsets):
        value = jnp.transpose(jnp.concatenate([part for index in block for part in rows_of(index)]))
        turned[0:8, :] = value[LANES - 8 :]
        turned[8 : LANES + 8, :] = value
        turned[LANES + 8 : LANES + 16, :] = value[:8]
        result = []
        for offset in offsets:
            total = None
            for j in range(PACKED):
                row = 8 + j * SEGMENT + offset
                value = turned[row : row + 8, :] + turned[row + 8 : row + 16, :]
                value = jnp.broadcast_to(jnp.sum(value, axis=0, keepdims=True), (8, LANES))
                total = value if total is None else jnp.where(row_of_block >= j, value, total)
            result.append(total)
        return result

    def lanes_of(value, place):
        return value if place == 0 else pltpu.roll(value, LANES - place * GROUPS, 1)

    (first,) = totals((0, 1, 2, 3), (0,))
    second, second_low, second_high = totals((4, 5, 6, 7), (0, -1, 1))
    third, third_low, third_high = totals((8, 9, 10, 11), (0, -1, 1))
    (fourth,) = totals((12, 12, 12, 12), (0,))
    cross = [lanes_of(first, place) for place in range(4)]
    cross += [second, lanes_of(third_low, 2), lanes_of(third_high, 3)]
    powers = [lanes_of(second, place) for place in (1, 2, 3)]
    powers += [third, lanes_of(third, 1), lanes_of(second_low, 1), lanes_of(second_high, 1)]
    kernel_power = fourth * (1.0 / CELLS) + EPSILON
    result = []
    for index in range(7):
        mean = cross[index] * (1.0 / CELLS)
        window_power = powers[index] * (1.0 / CELLS) + EPSILON
        result.append(math.sqrt(CELLS) * mean / jnp.sqrt(kernel_power * window_power))
    moves = []
    for axis in range(3):
        lower = result[1 + 2 * axis]
        upper = result[2 + 2 * axis]
        curvature = jnp.maximum(2.0 * result[0] - lower - upper, 1.0)
        moves.append((upper - lower) / (2.0 * curvature))
    for bx in range(BX):
        for index in range(7):
            value = pltpu.roll(result[index], (LANES - bx * BY) % LANES, 1)
            scores[index, 0, bx] = value[:PACKED, :BY]
        for axis in range(3):
            value = pltpu.roll(moves[axis], (LANES - bx * BY) % LANES, 1)
            cells = shift_cells[axis, 0, bx].astype(jnp.float32)
            displacement[axis, 0, bx] = cells + value[:PACKED, :BY]


def on_chip(count):
    return [pl.BlockSpec(memory_space=pltpu.VMEM)] * count


def pinned(array):
    return pltpu.with_memory_space_constraint(array, pltpu.VMEM)


def in_hbm(array):
    return pltpu.with_memory_space_constraint(array, pltpu.HBM)


def per_device(element_data, migration, column_gain, depth_gain, coarse_shift, reference_frame):
    elements_here, frames_here, depth = element_data.shape
    depth_here = depth_gain.shape[0]
    slabs = lax.axis_size("slab")
    frames = lax.axis_size("frame")
    elements = elements_here * slabs
    assert frames_here == 1 and depth_here == STEP
    chosen = reference_frame[0]
    frame = lax.axis_index("frame")
    slab = lax.axis_index("slab")
    own_data = element_data.reshape(elements_here, depth)
    scalars = pl.BlockSpec(memory_space=pltpu.SMEM)

    if elements_here == LANES:
        windows = pl.pallas_call(
            window_rows,
            in_specs=[pl.BlockSpec(memory_space=pltpu.HBM)] * 2,
            out_specs=on_chip(1)[0],
            out_shape=jax.ShapeDtypeStruct((slabs, WINDOW, LANES), jnp.bfloat16),
            scratch_shapes=[
                pltpu.VMEM((depth // LANES, LANES, LANES), jnp.bfloat16),
                pltpu.VMEM((1, STEP), jnp.float32),
                pltpu.VMEM((EDGE, LANES), jnp.float32),
                pltpu.SemaphoreType.DMA((depth // LANES + 1,)),
            ],
            compiler_params=pltpu.CompilerParams(vmem_limit_bytes=4 << 20),
            name="window_rows",
        )(in_hbm(own_data), in_hbm(depth_gain.reshape(1, STEP)))
        own = lax.all_to_all(windows, "slab", split_axis=0, concat_axis=0, tiled=True)
        places = [slab + step & slabs - 1 for step in (-1, 0, 1)]
    else:
        turned = jnp.pad(own_data.T, ((EDGE, EDGE), (0, 0)))
        windows = jnp.stack([turned[i * STEP : i * STEP + WINDOW] for i in range(slabs)])
        own = lax.all_to_all(windows, "slab", split_axis=0, concat_axis=0, tiled=True)
        own = own.transpose(1, 0, 2).reshape(WINDOW, elements // LANES, LANES).transpose(1, 0, 2)
        ring = [(i, (i + 1) % slabs) for i in range(slabs)]
        left = lax.ppermute(depth_gain, "slab", ring)
        right = lax.ppermute(depth_gain, "slab", [(j, i) for i, j in ring])
        high = lambda value: lax.reduce_precision(value, 8, 7)
        for place, value in enumerate((left, depth_gain, right)):
            middle = high(value - high(value))
            note = jnp.stack([high(value), middle, value - high(value) - middle])
            own = own.at[place, :3, :STEP].set(note.astype(jnp.bfloat16))
        places = [0, 1, 2]

    places = [jnp.asarray(place, jnp.int32) for place in places]
    gain_table = column_gain.reshape(-1, LANES)
    turn = (0, 1, 2, 4, 3)
    shifts = coarse_shift.transpose(turn)
    own_shapes = [(SPREAD, LANES), (LX * LY, LANES), (LX * LY, LANES)]
    own_shapes += [(2, GROUPS * 8, LANES), (GROUPS * SUMS, LANES)]
    kernel_arrays = pl.pallas_call(
        own_kernels,
        in_specs=[scalars] + on_chip(1) + [pl.BlockSpec(memory_space=pltpu.HBM)] * 3,
        out_specs=on_chip(9),
        out_shape=[pltpu.VMEM(shape, jnp.float32) for shape in own_shapes]
        + [
            pltpu.VMEM((8, LANES), jnp.int32),
            pltpu.VMEM(shifts.shape, jnp.int32),
            pltpu.VMEM((LANES, LX * LY // LANES), jnp.float32),
            pltpu.VMEM(migration.shape, jnp.bfloat16),
        ],
        scratch_shapes=[
            pltpu.VMEM((2 * BX * PACKED, LANES), jnp.float32),
            pltpu.VMEM((LX * LY // LANES, LANES), jnp.float32),
            pltpu.SemaphoreType.DMA((LX // LOAD + 2,)),
        ],
        compiler_params=pltpu.CompilerParams(vmem_limit_bytes=16 << 20),
        name="own_kernels",
    )(jnp.stack(places), pinned(own), in_hbm(migration), in_hbm(gain_table), in_hbm(shifts))

    kept = own
    bit = 1
    while bit < frames // 2:
        received = lax.ppermute(kept, "frame", [(i, i ^ bit) for i in range(frames)])
        mine = (chosen ^ frame) & bit == 0
        kept = jnp.where(mine, kept, received)
        bit *= 2
    half = kept.shape[0] // 2
    received = [
        lax.ppermute(part, "frame", [(i, i ^ bit) for i in range(frames)])
        for part in (kept[:half], kept[half:])
    ]
    keep = ((chosen ^ frame) & (frames // 2) == 0).astype(jnp.int32)
    choice = jnp.stack([keep] + places)

    *kernel_arrays, staged = kernel_arrays
    partial = pl.pallas_call(
        reference_part,
        in_specs=[scalars] + on_chip(3),
        out_specs=on_chip(1)[0],
        out_shape=pltpu.VMEM((LX * LY, LANES), jnp.float32),
        compiler_params=pltpu.CompilerParams(vmem_limit_bytes=8 << 20),
        name="reference_part",
    )(choice, pinned(kept), pinned(received[0]), pinned(staged))

    shapes = [jax.ShapeDtypeStruct((n,) + shifts.shape[1:], jnp.float32) for n in (7, 3)]
    scores, displacement = pl.pallas_call(
        track,
        in_specs=[scalars] + on_chip(12),
        out_specs=on_chip(2),
        out_shape=shapes,
        scratch_shapes=[
            pltpu.VMEM((VOLUME, LANES), jnp.float32),
            pltpu.VMEM((12, GROUPS * SUMS, LANES), jnp.float32),
            pltpu.VMEM((LANES + 16, LANES), jnp.float32),
            pltpu.SMEM((8, LANES), jnp.int32),
            pltpu.SemaphoreType.DMA,
        ],
        compiler_params=pltpu.CompilerParams(vmem_limit_bytes=24 << 20),
        name="track",
    )(
        choice,
        pinned(kept),
        pinned(received[1]),
        *[pinned(array) for array in [partial, *kernel_arrays, staged]],
    )
    return scores.transpose(turn), displacement.transpose(turn)


def solution(mesh):
    blocks = P(None, "frame", None, None, "slab")
    placed = (P("slab", "frame", None), P(), P(), P("slab"), blocks, P())
    return jax.shard_map(
        per_device, mesh=mesh, in_specs=placed, out_specs=(blocks, blocks), check_vma=False
    )
```

```python
import functools
import math

import jax
import jax.numpy as jnp
from jax import lax
from jax.experimental import pallas as pl
from jax.experimental.pallas import tpu as pltpu
from jax.sharding import PartitionSpec as P

LX = 32
LY = 64
KX = 8
KY = 8
KZ = 16
CMAX = 8
MARGIN = CMAX + 1
EPSILON = 1e-05

LANES = 128
STEP = 64
EDGE = 16
WINDOW = STEP + 2 * EDGE
SEGMENT = 32
PACKED = STEP // KZ
BX = LX // KX
BY = LY // KY
GROUPS = BX * BY
NX = LX + 2 * MARGIN
NY = 89
KROWS = 145
SPREAD = LX * KROWS + 7
VOLUME = NX * NY + 6
SUMS = 9
CELLS = KX * KY * KZ
STRIP = 4
LOAD = 16


def pieces_of(value):
    high = value.astype(jnp.bfloat16).astype(jnp.float32)
    middle = (value - high).astype(jnp.bfloat16).astype(jnp.float32)
    return high, middle, value - high - middle


def window_rows(element_data, depth_gain, windows, held, gain, row, arrived):
    columns = element_data.shape[1] // LANES
    copies = [pltpu.make_async_copy(depth_gain, gain, arrived.at[columns])]
    for column in range(columns):
        part = element_data.at[:, column * LANES : (column + 1) * LANES]
        copies.append(pltpu.make_async_copy(part, held.at[column], arrived.at[column]))
    for copy in copies:
        copy.start()
    row[...] = jnp.zeros(row.shape, jnp.float32)
    copies[0].wait()
    for index, piece in enumerate(pieces_of(gain[...])):
        row[index : index + 1, :STEP] = piece
    note = row[...].astype(jnp.bfloat16)
    slabs = windows.shape[0]
    empty = jnp.zeros((EDGE, LANES), jnp.bfloat16)
    spare = lax.broadcasted_iota(jnp.int32, (EDGE, LANES), 0) < 3

    def put(slab, first, rows):
        if 0 <= slab < slabs:
            if first == 0:
                rows = jnp.where(spare, note, rows)
            windows[slab, first : first + EDGE, :] = rows

    put(0, 0, empty)
    put(slabs - 1, EDGE + STEP, empty)
    for column in range(columns):
        copies[1 + column].wait()
        turned = jnp.transpose(held[column])
        for unit in range(LANES // EDGE):
            slab, place = divmod(column * LANES + unit * EDGE, STEP)
            rows = turned[unit * EDGE : (unit + 1) * EDGE]
            put(slab, place + EDGE, rows)
            if place == STEP - EDGE:
                put(slab + 1, 0, rows)
            if place == 0:
                put(slab - 1, EDGE + STEP, rows)


def depth_row(choice, samples):
    lane = lax.broadcasted_iota(jnp.int32, (8, LANES), 1)

    def of(which):
        note = samples[choice[which], :EDGE, :].astype(jnp.float32)
        return jnp.broadcast_to(note[0:1] + note[1:2] + note[2:3], (8, LANES))

    row = pltpu.roll(of(2), EDGE, 1)
    row = jnp.where(lane < EDGE, pltpu.roll(of(1), (EDGE - STEP) % LANES, 1), row)
    return jnp.where(lane >= EDGE + STEP, pltpu.roll(of(3), EDGE + STEP, 1), row)


def migrated(right, migration, begin, end, first=0):
    rows = migration[begin // LOAD]
    shift = begin // LOAD * LOAD
    return lax.dot_general(
        rows[(begin - shift) * LY : (end - shift) * LY, first : first + right.shape[1]],
        right,
        (((1,), (1,)), ((), ())),
        preferred_element_type=jnp.float32,
    )


def finish(raw, columns, gains, store, begin, end):
    for x in range(begin, end):
        row = x * LY
        gain = columns[row % LANES : row % LANES + LY, row // LANES : row // LANES + 1]
        image = raw[(x - begin) * LY : (x - begin + 1) * LY]
        image = image * jnp.broadcast_to(gain, image.shape)
        store(x, (image * gains).astype(jnp.bfloat16).astype(jnp.float32))


def block_table(shifts, table, spread):
    j = lax.broadcasted_iota(jnp.int32, (PACKED, BY), 0)
    by = lax.broadcasted_iota(jnp.int32, (PACKED, BY), 1)
    spread[...] = jnp.zeros(spread.shape, jnp.float32)
    for bx in range(BX):
        first, second, third = (shifts[axis, 0, bx] for axis in range(3))
        start = (first + (bx * KX + MARGIN)) * NY + second + by * KY + MARGIN
        turn = (j * KZ + (LANES - EDGE) - third) & (LANES - 1)
        for index, value in enumerate((start, turn)):
            row = index * BX * PACKED + bx * PACKED
            spread[row : row + PACKED, :BY] = value.astype(jnp.float32)
    rows = BX * PACKED
    row = lax.broadcasted_iota(jnp.int32, (rows, LANES), 0)
    lane = lax.broadcasted_iota(jnp.int32, (rows, LANES), 1)
    for index in range(2):
        value = spread[index * rows : (index + 1) * rows, :]
        value = pltpu.roll(value, 0, 1, stride=BY, stride_axis=0)
        value = jnp.sum(jnp.where(lane // BY == row, value, 0.0), axis=0, keepdims=True)
        table[index : index + 1, :] = value.astype(jnp.int32)


def migration_part(own, source, part, arrived):
    copy = pltpu.make_async_copy(source.at[: part.shape[0], :], part, arrived)
    copy.start()
    copy.wait()


def own_kernels(
    choice,
    own,
    migration_low,
    migration_source,
    column_gain,
    shift_source,
    kernels,
    deeper,
    shallower,
    edges,
    powers,
    table,
    shifts,
    columns,
    migration_high,
    spread,
    gain_rows,
    arrived,
):
    copies = [
        pltpu.make_async_copy(column_gain, gain_rows, arrived.at[0]),
        pltpu.make_async_copy(shift_source, shifts, arrived.at[1]),
        pltpu.make_async_copy(
            migration_source.at[LOAD * LY :, :], migration_high, arrived.at[2]
        ),
    ]
    migration = (migration_low, migration_high)
    for copy in copies:
        copy.start()
    gap = jnp.zeros((SEGMENT - KZ, migration_low.shape[1]), jnp.bfloat16)
    rows = []
    for j in range(PACKED):
        cells = slice(EDGE + j * KZ, EDGE + (j + 1) * KZ)
        pieces = [own[b, cells, :] for b in range(own.shape[0])]
        rows += [jnp.concatenate(pieces, axis=1), gap]
    lane = lax.broadcasted_iota(jnp.int32, (8, LANES), 1)
    note = own[choice[1], :EDGE, :].astype(jnp.float32)
    row = jnp.broadcast_to(note[0:1] + note[1:2] + note[2:3], (8, LANES))
    gains = row
    for j in range(1, PACKED):
        gains = jnp.where(lane >= j * SEGMENT, pltpu.roll(row, j * KZ, 1), gains)
    for x in range(LX):
        for by in range(BY + 1):
            kernels[x * KROWS + by * 16 : x * KROWS + by * 16 + 8, :] = jnp.zeros((8, LANES))

    def store(x, image):
        for by in range(BY):
            row = x * KROWS + 8 + by * 16
            kernel = image[by * KY : (by + 1) * KY]
            kernels[row : row + 8, :] = kernel
            row = x * LY + by * KY
            shallower[row : row + 8, :] = pltpu.roll(kernel, LANES - 1, 1)
            deeper[row : row + 8, :] = pltpu.roll(kernel, 1, 1)

    right = jnp.concatenate(rows)
    copies[0].wait()
    columns[...] = jnp.transpose(gain_rows[...])
    copies[1].wait()
    block_table(shifts, table, spread)
    for begin in range(0, LX, LOAD):
        if begin:
            copies[2].wait()
        for x in range(begin, begin + LOAD, STRIP):
            raw = migrated(right, migration, x, x + STRIP)
            finish(raw, columns, gains[:1], store, x, x + STRIP)
    for g in range(GROUPS):
        base = g // BY * KX * KROWS + g % BY * 16 + 8
        power = None
        for x in range(KX):
            kernel = kernels[base + x * KROWS : base + x * KROWS + 8, :]
            power = kernel * kernel if power is None else power + kernel * kernel
        powers[g * SUMS : g * SUMS + 8, :] = power
        for index, row in enumerate((base, base + KY - 1)):
            edges[index, g * 8 : g * 8 + 8, :] = kernels[pl.ds(row, 8, stride=KROWS), :]


def reference_samples(choice, kept, received, first):
    keep = choice[0] == 1
    blocks = received.shape[0]
    pieces = [jnp.where(keep, kept[first + b], received[b]) for b in range(blocks)]
    spare = jnp.zeros((LANES - WINDOW, blocks * LANES), jnp.bfloat16)
    return jnp.concatenate([jnp.concatenate(pieces, axis=1), spare])


def reference_part(choice, kept, received, migration_low, migration_high, partial):
    migration = (migration_low, migration_high)
    right = reference_samples(choice, kept, received, 0)
    for x in range(0, LX, STRIP):
        partial[x * LY : (x + STRIP) * LY, :] = migrated(right, migration, x, x + STRIP)


def track(
    choice,
    kept,
    received,
    partial,
    kernels,
    deeper,
    shallower,
    edges,
    kernel_powers,
    table,
    shift_cells,
    columns,
    migration_high,
    migration_low,
    scores,
    displacement,
    volume,
    sums,
    turned,
    block,
    arrived,
):
    positions = pltpu.make_async_copy(table, block, arrived)
    positions.start()

    def store(x, image):
        base = (x + MARGIN) * NY + MARGIN
        volume[base : base + LY, :] = image

    migration = (migration_low, migration_high)
    first = kept.shape[0] - received.shape[0]
    right = reference_samples(choice, kept, received, first)
    gains = depth_row(choice, kept)[:1]
    for x in range(0, LX, STRIP):
        raw = partial[x * LY : (x + STRIP) * LY, :]
        raw = raw + migrated(right, migration, x, x + STRIP, first * LANES)
        finish(raw, columns, gains, store, x, x + STRIP)
    zero = jnp.zeros((NY, LANES), jnp.float32)
    for x in list(range(MARGIN)) + list(range(LX + MARGIN, NX)):
        volume[x * NY : (x + 1) * NY, :] = zero
    for x in range(MARGIN, LX + MARGIN):
        volume[x * NY : x * NY + MARGIN, :] = zero[:MARGIN]
        volume[x * NY + MARGIN + LY : (x + 1) * NY, :] = zero[: NY - MARGIN - LY]
    positions.wait()

    lane = lax.broadcasted_iota(jnp.int32, (16, LANES), 1)
    segment = [((lane + 8) & (LANES - 1)) // SEGMENT == j for j in range(PACKED)]
    row_number = lax.broadcasted_iota(jnp.int32, (8, LANES), 0)

    def group(bx, by):
        g = bx * BY + by
        number = [(bx * PACKED + j) * BY + by for j in range(PACKED)]
        starts = [block[0, n] for n in number]
        turns = [block[1, n] for n in number]

        def gather(offsets, stride=None):
            value = None
            for j in range(PACKED):
                pair = []
                for offset in offsets:
                    if stride is None:
                        pair.append(volume[pl.ds(starts[j] + offset, 8), :])
                    else:
                        pair.append(volume[pl.ds(starts[j] + offset, 8, stride=stride), :])
                rows = jnp.concatenate(pair).astype(jnp.bfloat16)
                rows = pltpu.roll(rows, turns[j], 1)
                value = rows if value is None else jnp.where(segment[j], rows, value)
            value = value.astype(jnp.float32)
            return [value[:8], value[8:]]

        window = []
        for x in range(-1, KX, 2):
            window += gather((x * NY, (x + 1) * NY))
        before, after = gather((-1, KY), NY)
        square = [value * value for value in window]
        middle = square[2]
        for x in range(3, KX):
            middle = middle + square[x]
        pair_low = square[0] + square[1]
        pair_high = square[KX] + square[KX + 1]
        center = middle + (square[1] + square[KX])
        cross = [None] * 7

        def add(index, value):
            cross[index] = value if cross[index] is None else cross[index] + value

        base = bx * KX * KROWS + by * 16 + 8
        flat = bx * KX * LY + by * KY
        for x in range(KX):
            row = base + x * KROWS
            kernel = kernels[pl.ds(row, 8), :]
            add(0, kernel * window[x + 1])
            add(1, kernel * window[x])
            add(2, kernel * window[x + 2])
            add(3, kernels[pl.ds(row + 1, 8), :] * window[x + 1])
            add(4, kernels[pl.ds(row - 1, 8), :] * window[x + 1])
            aligned = pl.ds(flat + x * LY, 8)
            add(5, shallower[aligned, :] * window[x + 1])
            add(6, deeper[aligned, :] * window[x + 1])
        rows = pl.ds(g * 8, 8)
        add(3, edges[0, rows, :] * before)
        add(4, edges[1, rows, :] * after)
        low = jnp.where(row_number < KY - 1, center, 0.0) + before * before
        high = jnp.where(row_number > 0, center, 0.0) + after * after
        held = cross[:5] + [center, middle + pair_low, middle + pair_high]
        held += [low, high, cross[5], cross[6]]
        for index, value in enumerate(held):
            sums[index, pl.ds(g * SUMS, 8), :] = value

    for bx in range(BX):
        for by in range(BY):
            group(bx, by)

    def rows_of(index):
        parts = []
        for bx in range(BX):
            value = None
            for y in range(KY):
                place = pl.ds(bx * BY * SUMS + y, BY, stride=SUMS)
                rows = sums[index, place, :] if index < 12 else kernel_powers[place, :]
                value = rows if value is None else value + rows
            parts.append(value)
        return parts

    row_of_block = lax.broadcasted_iota(jnp.int32, (8, LANES), 0)

    def totals(block, offsets):
        value = jnp.transpose(jnp.concatenate([part for index in block for part in rows_of(index)]))
        turned[0:8, :] = value[LANES - 8 :]
        turned[8 : LANES + 8, :] = value
        turned[LANES + 8 : LANES + 16, :] = value[:8]
        result = []
        for offset in offsets:
            total = None
            for j in range(PACKED):
                row = 8 + j * SEGMENT + offset
                value = turned[row : row + 8, :] + turned[row + 8 : row + 16, :]
                value = jnp.broadcast_to(jnp.sum(value, axis=0, keepdims=True), (8, LANES))
                total = value if total is None else jnp.where(row_of_block >= j, value, total)
            result.append(total)
        return result

    def lanes_of(value, place):
        return value if place == 0 else pltpu.roll(value, LANES - place * GROUPS, 1)

    (first,) = totals((0, 1, 2, 3), (0,))
    second, second_low, second_high = totals((4, 5, 6, 7), (0, -1, 1))
    third, third_low, third_high = totals((8, 9, 10, 11), (0, -1, 1))
    (fourth,) = totals((12, 12, 12, 12), (0,))
    cross = [lanes_of(first, place) for place in range(4)]
    cross += [second, lanes_of(third_low, 2), lanes_of(third_high, 3)]
    powers = [lanes_of(second, place) for place in (1, 2, 3)]
    powers += [third, lanes_of(third, 1), lanes_of(second_low, 1), lanes_of(second_high, 1)]
    kernel_power = fourth * (1.0 / CELLS) + EPSILON
    result = []
    for index in range(7):
        mean = cross[index] * (1.0 / CELLS)
        window_power = powers[index] * (1.0 / CELLS) + EPSILON
        result.append(math.sqrt(CELLS) * mean / jnp.sqrt(kernel_power * window_power))
    moves = []
    for axis in range(3):
        lower = result[1 + 2 * axis]
        upper = result[2 + 2 * axis]
        curvature = jnp.maximum(2.0 * result[0] - lower - upper, 1.0)
        moves.append((upper - lower) / (2.0 * curvature))
    for bx in range(BX):
        for index in range(7):
            value = pltpu.roll(result[index], (LANES - bx * BY) % LANES, 1)
            scores[index, 0, bx] = value[:PACKED, :BY]
        for axis in range(3):
            value = pltpu.roll(moves[axis], (LANES - bx * BY) % LANES, 1)
            cells = shift_cells[axis, 0, bx].astype(jnp.float32)
            displacement[axis, 0, bx] = cells + value[:PACKED, :BY]


def on_chip(count):
    return [pl.BlockSpec(memory_space=pltpu.VMEM)] * count


def pinned(array):
    return pltpu.with_memory_space_constraint(array, pltpu.VMEM)


def in_hbm(array):
    return pltpu.with_memory_space_constraint(array, pltpu.HBM)


def per_device(element_data, migration, column_gain, depth_gain, coarse_shift, reference_frame):
    elements_here, frames_here, depth = element_data.shape
    depth_here = depth_gain.shape[0]
    slabs = lax.axis_size("slab")
    frames = lax.axis_size("frame")
    elements = elements_here * slabs
    assert frames_here == 1 and depth_here == STEP
    chosen = reference_frame[0]
    frame = lax.axis_index("frame")
    slab = lax.axis_index("slab")
    own_data = element_data.reshape(elements_here, depth)
    scalars = pl.BlockSpec(memory_space=pltpu.SMEM)

    if elements_here == LANES:
        windows = pl.pallas_call(
            window_rows,
            in_specs=[pl.BlockSpec(memory_space=pltpu.HBM)] * 2,
            out_specs=on_chip(1)[0],
            out_shape=jax.ShapeDtypeStruct((slabs, WINDOW, LANES), jnp.bfloat16),
            scratch_shapes=[
                pltpu.VMEM((depth // LANES, LANES, LANES), jnp.bfloat16),
                pltpu.VMEM((1, STEP), jnp.float32),
                pltpu.VMEM((EDGE, LANES), jnp.float32),
                pltpu.SemaphoreType.DMA((depth // LANES + 1,)),
            ],
            compiler_params=pltpu.CompilerParams(vmem_limit_bytes=4 << 20),
            name="window_rows",
        )(in_hbm(own_data), in_hbm(depth_gain.reshape(1, STEP)))
        own = lax.all_to_all(windows, "slab", split_axis=0, concat_axis=0, tiled=True)
        places = [slab + step & slabs - 1 for step in (-1, 0, 1)]
    else:
        turned = jnp.pad(own_data.T, ((EDGE, EDGE), (0, 0)))
        windows = jnp.stack([turned[i * STEP : i * STEP + WINDOW] for i in range(slabs)])
        own = lax.all_to_all(windows, "slab", split_axis=0, concat_axis=0, tiled=True)
        own = own.transpose(1, 0, 2).reshape(WINDOW, elements // LANES, LANES).transpose(1, 0, 2)
        ring = [(i, (i + 1) % slabs) for i in range(slabs)]
        left = lax.ppermute(depth_gain, "slab", ring)
        right = lax.ppermute(depth_gain, "slab", [(j, i) for i, j in ring])
        high = lambda value: lax.reduce_precision(value, 8, 7)
        for place, value in enumerate((left, depth_gain, right)):
            middle = high(value - high(value))
            note = jnp.stack([high(value), middle, value - high(value) - middle])
            own = own.at[place, :3, :STEP].set(note.astype(jnp.bfloat16))
        places = [0, 1, 2]

    places = [jnp.asarray(place, jnp.int32) for place in places]
    gain_table = column_gain.reshape(-1, LANES)
    turn = (0, 1, 2, 4, 3)
    shifts = coarse_shift.transpose(turn)
    own_shapes = [(SPREAD, LANES), (LX * LY, LANES), (LX * LY, LANES)]
    own_shapes += [(2, GROUPS * 8, LANES), (GROUPS * SUMS, LANES)]
    low = pl.pallas_call(
        migration_part,
        in_specs=on_chip(1) + [pl.BlockSpec(memory_space=pltpu.HBM)],
        out_specs=on_chip(1)[0],
        out_shape=pltpu.VMEM((LOAD * LY, elements), jnp.bfloat16),
        scratch_shapes=[pltpu.SemaphoreType.DMA],
        compiler_params=pltpu.CompilerParams(vmem_limit_bytes=4 << 20),
        name="migration_part",
    )(pinned(own), in_hbm(migration))
    kept = own
    bit = 1
    while bit < frames // 2:
        received = lax.ppermute(kept, "frame", [(i, i ^ bit) for i in range(frames)])
        mine = (chosen ^ frame) & bit == 0
        kept = jnp.where(mine, kept, received)
        bit *= 2
    kept, low = lax.optimization_barrier((kept, low))
    half = kept.shape[0] // 2
    received = [
        lax.ppermute(part, "frame", [(i, i ^ bit) for i in range(frames)])
        for part in (kept[:half], kept[half:])
    ]
    kernel_arrays = pl.pallas_call(
        own_kernels,
        in_specs=[scalars] + on_chip(2) + [pl.BlockSpec(memory_space=pltpu.HBM)] * 3,
        out_specs=on_chip(9),
        out_shape=[pltpu.VMEM(shape, jnp.float32) for shape in own_shapes]
        + [
            pltpu.VMEM((8, LANES), jnp.int32),
            pltpu.VMEM(shifts.shape, jnp.int32),
            pltpu.VMEM((LANES, LX * LY // LANES), jnp.float32),
            pltpu.VMEM((LX * LY - LOAD * LY, elements), jnp.bfloat16),
        ],
        scratch_shapes=[
            pltpu.VMEM((2 * BX * PACKED, LANES), jnp.float32),
            pltpu.VMEM((LX * LY // LANES, LANES), jnp.float32),
            pltpu.SemaphoreType.DMA((3,)),
        ],
        compiler_params=pltpu.CompilerParams(vmem_limit_bytes=16 << 20),
        name="own_kernels",
    )(
        jnp.stack(places),
        pinned(own),
        pinned(low),
        in_hbm(migration),
        in_hbm(gain_table),
        in_hbm(shifts),
    )

    keep = ((chosen ^ frame) & (frames // 2) == 0).astype(jnp.int32)
    choice = jnp.stack([keep] + places)

    *kernel_arrays, staged = kernel_arrays
    partial = pl.pallas_call(
        reference_part,
        in_specs=[scalars] + on_chip(4),
        out_specs=on_chip(1)[0],
        out_shape=pltpu.VMEM((LX * LY, LANES), jnp.float32),
        compiler_params=pltpu.CompilerParams(vmem_limit_bytes=8 << 20),
        name="reference_part",
    )(choice, pinned(kept), pinned(received[0]), pinned(low), pinned(staged))

    shapes = [jax.ShapeDtypeStruct((n,) + shifts.shape[1:], jnp.float32) for n in (7, 3)]
    scores, displacement = pl.pallas_call(
        track,
        in_specs=[scalars] + on_chip(13),
        out_specs=on_chip(2),
        out_shape=shapes,
        scratch_shapes=[
            pltpu.VMEM((VOLUME, LANES), jnp.float32),
            pltpu.VMEM((12, GROUPS * SUMS, LANES), jnp.float32),
            pltpu.VMEM((LANES + 16, LANES), jnp.float32),
            pltpu.SMEM((8, LANES), jnp.int32),
            pltpu.SemaphoreType.DMA,
        ],
        compiler_params=pltpu.CompilerParams(vmem_limit_bytes=24 << 20),
        name="track",
    )(
        choice,
        pinned(kept),
        pinned(received[1]),
        *[pinned(array) for array in [partial, *kernel_arrays, staged, low]],
    )
    return scores.transpose(turn), displacement.transpose(turn)


def solution(mesh):
    blocks = P(None, "frame", None, None, "slab")
    placed = (P("slab", "frame", None), P(), P(), P("slab"), blocks, P())
    return jax.shard_map(
        per_device, mesh=mesh, in_specs=placed, out_specs=(blocks, blocks), check_vma=False
    )
```

```python
import functools
import math

import jax
import jax.numpy as jnp
from jax import lax
from jax.experimental import pallas as pl
from jax.experimental.pallas import tpu as pltpu
from jax.sharding import PartitionSpec as P

LX = 32
LY = 64
KX = 8
KY = 8
KZ = 16
CMAX = 8
MARGIN = CMAX + 1
EPSILON = 1e-05

LANES = 128
STEP = 64
EDGE = 16
WINDOW = STEP + 2 * EDGE
SEGMENT = 32
PACKED = STEP // KZ
BX = LX // KX
BY = LY // KY
GROUPS = BX * BY
NX = LX + 2 * MARGIN
NY = 89
KROWS = 145
SPREAD = LX * KROWS + 7
VOLUME = NX * NY + 6
SUMS = 9
CELLS = KX * KY * KZ
STRIP = 4
LOAD = 16


def pieces_of(value):
    high = value.astype(jnp.bfloat16).astype(jnp.float32)
    middle = (value - high).astype(jnp.bfloat16).astype(jnp.float32)
    return high, middle, value - high - middle


def window_rows(element_data, depth_gain, windows, held, gain, row, arrived):
    columns = element_data.shape[1] // LANES
    copies = [pltpu.make_async_copy(depth_gain, gain, arrived.at[columns])]
    for column in range(columns):
        part = element_data.at[:, column * LANES : (column + 1) * LANES]
        copies.append(pltpu.make_async_copy(part, held.at[column], arrived.at[column]))
    for copy in copies:
        copy.start()
    row[...] = jnp.zeros(row.shape, jnp.float32)
    copies[0].wait()
    for index, piece in enumerate(pieces_of(gain[...])):
        row[index : index + 1, :STEP] = piece
    note = row[...].astype(jnp.bfloat16)
    slabs = windows.shape[0]
    empty = jnp.zeros((EDGE, LANES), jnp.bfloat16)
    spare = lax.broadcasted_iota(jnp.int32, (EDGE, LANES), 0) < 3

    def put(slab, first, rows):
        if 0 <= slab < slabs:
            if first == 0:
                rows = jnp.where(spare, note, rows)
            windows[slab, first : first + EDGE, :] = rows

    put(0, 0, empty)
    put(slabs - 1, EDGE + STEP, empty)
    for column in range(columns):
        copies[1 + column].wait()
        turned = jnp.transpose(held[column])
        for unit in range(LANES // EDGE):
            slab, place = divmod(column * LANES + unit * EDGE, STEP)
            rows = turned[unit * EDGE : (unit + 1) * EDGE]
            put(slab, place + EDGE, rows)
            if place == STEP - EDGE:
                put(slab + 1, 0, rows)
            if place == 0:
                put(slab - 1, EDGE + STEP, rows)


def depth_row(choice, samples):
    lane = lax.broadcasted_iota(jnp.int32, (8, LANES), 1)

    def of(which):
        note = samples[choice[which], :EDGE, :].astype(jnp.float32)
        return jnp.broadcast_to(note[0:1] + note[1:2] + note[2:3], (8, LANES))

    row = pltpu.roll(of(2), EDGE, 1)
    row = jnp.where(lane < EDGE, pltpu.roll(of(1), (EDGE - STEP) % LANES, 1), row)
    return jnp.where(lane >= EDGE + STEP, pltpu.roll(of(3), EDGE + STEP, 1), row)


def migrate(right, migration, columns, gains, store, begin, end):
    raw = lax.dot_general(
        migration[begin * LY : end * LY, :],
        right,
        (((1,), (1,)), ((), ())),
        preferred_element_type=jnp.float32,
    )
    for x in range(begin, end):
        row = x * LY
        gain = columns[row % LANES : row % LANES + LY, row // LANES : row // LANES + 1]
        image = raw[(x - begin) * LY : (x - begin + 1) * LY]
        image = image * jnp.broadcast_to(gain, image.shape)
        store(x, (image * gains).astype(jnp.bfloat16).astype(jnp.float32))


def block_table(shifts, table, spread):
    j = lax.broadcasted_iota(jnp.int32, (PACKED, BY), 0)
    by = lax.broadcasted_iota(jnp.int32, (PACKED, BY), 1)
    spread[...] = jnp.zeros(spread.shape, jnp.float32)
    for bx in range(BX):
        first, second, third = (shifts[axis, 0, bx] for axis in range(3))
        start = (first + (bx * KX + MARGIN)) * NY + second + by * KY + MARGIN
        turn = (j * KZ + (LANES - EDGE) - third) & (LANES - 1)
        for index, value in enumerate((start, turn)):
            row = index * BX * PACKED + bx * PACKED
            spread[row : row + PACKED, :BY] = value.astype(jnp.float32)
    rows = BX * PACKED
    row = lax.broadcasted_iota(jnp.int32, (rows, LANES), 0)
    lane = lax.broadcasted_iota(jnp.int32, (rows, LANES), 1)
    for index in range(2):
        value = spread[index * rows : (index + 1) * rows, :]
        value = pltpu.roll(value, 0, 1, stride=BY, stride_axis=0)
        value = jnp.sum(jnp.where(lane // BY == row, value, 0.0), axis=0, keepdims=True)
        table[index : index + 1, :] = value.astype(jnp.int32)


def own_kernels(
    choice,
    own,
    migration_source,
    column_gain,
    shift_source,
    kernels,
    deeper,
    shallower,
    edges,
    powers,
    table,
    shifts,
    columns,
    migration,
    spread,
    gain_rows,
    arrived,
):
    strips = [(x, x + LOAD) for x in range(0, LX, LOAD)]
    copies = [
        pltpu.make_async_copy(column_gain, gain_rows, arrived.at[len(strips)]),
        pltpu.make_async_copy(shift_source, shifts, arrived.at[len(strips) + 1]),
    ]
    for index, (begin, end) in enumerate(strips):
        rows = pl.ds(begin * LY, (end - begin) * LY)
        copies.append(
            pltpu.make_async_copy(
                migration_source.at[rows, :], migration.at[rows, :], arrived.at[index]
            )
        )
    for copy in copies:
        copy.start()
    gap = jnp.zeros((SEGMENT - KZ, migration.shape[1]), jnp.bfloat16)
    rows = []
    for j in range(PACKED):
        cells = slice(EDGE + j * KZ, EDGE + (j + 1) * KZ)
        pieces = [own[b, cells, :] for b in range(own.shape[0])]
        rows += [jnp.concatenate(pieces, axis=1), gap]
    lane = lax.broadcasted_iota(jnp.int32, (8, LANES), 1)
    note = own[choice[1], :EDGE, :].astype(jnp.float32)
    row = jnp.broadcast_to(note[0:1] + note[1:2] + note[2:3], (8, LANES))
    gains = row
    for j in range(1, PACKED):
        gains = jnp.where(lane >= j * SEGMENT, pltpu.roll(row, j * KZ, 1), gains)
    for x in range(LX):
        for by in range(BY + 1):
            kernels[x * KROWS + by * 16 : x * KROWS + by * 16 + 8, :] = jnp.zeros((8, LANES))

    def store(x, image):
        for by in range(BY):
            row = x * KROWS + 8 + by * 16
            kernel = image[by * KY : (by + 1) * KY]
            kernels[row : row + 8, :] = kernel
            row = x * LY + by * KY
            shallower[row : row + 8, :] = pltpu.roll(kernel, LANES - 1, 1)
            deeper[row : row + 8, :] = pltpu.roll(kernel, 1, 1)

    right = jnp.concatenate(rows)
    copies[0].wait()
    columns[...] = jnp.transpose(gain_rows[...])
    copies[1].wait()
    block_table(shifts, table, spread)
    for copy, (begin, end) in zip(copies[2:], strips):
        copy.wait()
        migrate(right, migration, columns, gains[:1], store, begin, end)
    for g in range(GROUPS):
        base = g // BY * KX * KROWS + g % BY * 16 + 8
        power = None
        for x in range(KX):
            kernel = kernels[base + x * KROWS : base + x * KROWS + 8, :]
            power = kernel * kernel if power is None else power + kernel * kernel
        powers[g * SUMS : g * SUMS + 8, :] = power
        for index, row in enumerate((base, base + KY - 1)):
            edges[index, g * 8 : g * 8 + 8, :] = kernels[pl.ds(row, 8, stride=KROWS), :]


def track(
    choice,
    kept,
    received,
    kernels,
    deeper,
    shallower,
    edges,
    kernel_powers,
    table,
    shift_cells,
    columns,
    migration,
    scores,
    displacement,
    volume,
    sums,
    turned,
    block,
    arrived,
):
    positions = pltpu.make_async_copy(table, block, arrived)
    positions.start()
    keep = choice[0] == 1
    def store(x, image):
        base = (x + MARGIN) * NY + MARGIN
        volume[base : base + LY, :] = image

    pieces = [jnp.where(keep, kept[b], received[b]) for b in range(kept.shape[0])]
    spare = jnp.zeros((LANES - WINDOW, migration.shape[1]), jnp.bfloat16)
    right = jnp.concatenate([jnp.concatenate(pieces, axis=1), spare])
    gains = depth_row(choice, kept)[:1]

    lane = lax.broadcasted_iota(jnp.int32, (16, LANES), 1)
    segment = [((lane + 8) & (LANES - 1)) // SEGMENT == j for j in range(PACKED)]
    row_number = lax.broadcasted_iota(jnp.int32, (8, LANES), 0)

    def group(bx, by):
        g = bx * BY + by
        number = [(bx * PACKED + j) * BY + by for j in range(PACKED)]
        starts = [block[0, n] for n in number]
        turns = [block[1, n] for n in number]

        def gather(offsets, stride=None):
            value = None
            for j in range(PACKED):
                pair = []
                for offset in offsets:
                    if stride is None:
                        pair.append(volume[pl.ds(starts[j] + offset, 8), :])
                    else:
                        pair.append(volume[pl.ds(starts[j] + offset, 8, stride=stride), :])
                rows = jnp.concatenate(pair).astype(jnp.bfloat16)
                rows = pltpu.roll(rows, turns[j], 1)
                value = rows if value is None else jnp.where(segment[j], rows, value)
            value = value.astype(jnp.float32)
            return [value[:8], value[8:]]

        window = []
        for x in range(-1, KX, 2):
            window += gather((x * NY, (x + 1) * NY))
        before, after = gather((-1, KY), NY)
        square = [value * value for value in window]
        middle = square[2]
        for x in range(3, KX):
            middle = middle + square[x]
        pair_low = square[0] + square[1]
        pair_high = square[KX] + square[KX + 1]
        center = middle + (square[1] + square[KX])
        cross = [None] * 7

        def add(index, value):
            cross[index] = value if cross[index] is None else cross[index] + value

        base = bx * KX * KROWS + by * 16 + 8
        flat = bx * KX * LY + by * KY
        for x in range(KX):
            row = base + x * KROWS
            kernel = kernels[pl.ds(row, 8), :]
            add(0, kernel * window[x + 1])
            add(1, kernel * window[x])
            add(2, kernel * window[x + 2])
            add(3, kernels[pl.ds(row + 1, 8), :] * window[x + 1])
            add(4, kernels[pl.ds(row - 1, 8), :] * window[x + 1])
            aligned = pl.ds(flat + x * LY, 8)
            add(5, shallower[aligned, :] * window[x + 1])
            add(6, deeper[aligned, :] * window[x + 1])
        rows = pl.ds(g * 8, 8)
        add(3, edges[0, rows, :] * before)
        add(4, edges[1, rows, :] * after)
        low = jnp.where(row_number < KY - 1, center, 0.0) + before * before
        high = jnp.where(row_number > 0, center, 0.0) + after * after
        held = cross[:5] + [center, middle + pair_low, middle + pair_high]
        held += [low, high, cross[5], cross[6]]
        for index, value in enumerate(held):
            sums[index, pl.ds(g * SUMS, 8), :] = value

    for x in range(0, LX, STRIP):
        migrate(right, migration, columns, gains, store, x, x + STRIP)
    zero = jnp.zeros((NY, LANES), jnp.float32)
    for x in list(range(MARGIN)) + list(range(LX + MARGIN, NX)):
        volume[x * NY : (x + 1) * NY, :] = zero
    for x in range(MARGIN, LX + MARGIN):
        volume[x * NY : x * NY + MARGIN, :] = zero[:MARGIN]
        volume[x * NY + MARGIN + LY : (x + 1) * NY, :] = zero[: NY - MARGIN - LY]
    positions.wait()
    for bx in range(BX):
        for by in range(BY):
            group(bx, by)

    def rows_of(index):
        parts = []
        for bx in range(BX):
            value = None
            for y in range(KY):
                place = pl.ds(bx * BY * SUMS + y, BY, stride=SUMS)
                rows = sums[index, place, :] if index < 12 else kernel_powers[place, :]
                value = rows if value is None else value + rows
            parts.append(value)
        return parts

    row_of_block = lax.broadcasted_iota(jnp.int32, (8, LANES), 0)

    def totals(block, offsets):
        value = jnp.transpose(jnp.concatenate([part for index in block for part in rows_of(index)]))
        turned[0:8, :] = value[LANES - 8 :]
        turned[8 : LANES + 8, :] = value
        turned[LANES + 8 : LANES + 16, :] = value[:8]
        result = []
        for offset in offsets:
            total = None
            for j in range(PACKED):
                row = 8 + j * SEGMENT + offset
                value = turned[row : row + 8, :] + turned[row + 8 : row + 16, :]
                value = jnp.broadcast_to(jnp.sum(value, axis=0, keepdims=True), (8, LANES))
                total = value if total is None else jnp.where(row_of_block >= j, value, total)
            result.append(total)
        return result

    def lanes_of(value, place):
        return value if place == 0 else pltpu.roll(value, LANES - place * GROUPS, 1)

    (first,) = totals((0, 1, 2, 3), (0,))
    second, second_low, second_high = totals((4, 5, 6, 7), (0, -1, 1))
    third, third_low, third_high = totals((8, 9, 10, 11), (0, -1, 1))
    (fourth,) = totals((12, 12, 12, 12), (0,))
    cross = [lanes_of(first, place) for place in range(4)]
    cross += [second, lanes_of(third_low, 2), lanes_of(third_high, 3)]
    powers = [lanes_of(second, place) for place in (1, 2, 3)]
    powers += [third, lanes_of(third, 1), lanes_of(second_low, 1), lanes_of(second_high, 1)]
    kernel_power = fourth * (1.0 / CELLS) + EPSILON
    result = []
    for index in range(7):
        mean = cross[index] * (1.0 / CELLS)
        window_power = powers[index] * (1.0 / CELLS) + EPSILON
        result.append(math.sqrt(CELLS) * mean / jnp.sqrt(kernel_power * window_power))
    moves = []
    for axis in range(3):
        lower = result[1 + 2 * axis]
        upper = result[2 + 2 * axis]
        curvature = jnp.maximum(2.0 * result[0] - lower - upper, 1.0)
        moves.append((upper - lower) / (2.0 * curvature))
    for bx in range(BX):
        for index in range(7):
            value = pltpu.roll(result[index], (LANES - bx * BY) % LANES, 1)
            scores[index, 0, bx] = value[:PACKED, :BY]
        for axis in range(3):
            value = pltpu.roll(moves[axis], (LANES - bx * BY) % LANES, 1)
            cells = shift_cells[axis, 0, bx].astype(jnp.float32)
            displacement[axis, 0, bx] = cells + value[:PACKED, :BY]


def on_chip(count):
    return [pl.BlockSpec(memory_space=pltpu.VMEM)] * count


def pinned(array):
    return pltpu.with_memory_space_constraint(array, pltpu.VMEM)


def in_hbm(array):
    return pltpu.with_memory_space_constraint(array, pltpu.HBM)


def per_device(element_data, migration, column_gain, depth_gain, coarse_shift, reference_frame):
    elements_here, frames_here, depth = element_data.shape
    depth_here = depth_gain.shape[0]
    slabs = lax.axis_size("slab")
    frames = lax.axis_size("frame")
    elements = elements_here * slabs
    assert frames_here == 1 and depth_here == STEP
    chosen = reference_frame[0]
    frame = lax.axis_index("frame")
    slab = lax.axis_index("slab")
    own_data = element_data.reshape(elements_here, depth)
    scalars = pl.BlockSpec(memory_space=pltpu.SMEM)

    if elements_here == LANES:
        windows = pl.pallas_call(
            window_rows,
            in_specs=[pl.BlockSpec(memory_space=pltpu.HBM)] * 2,
            out_specs=on_chip(1)[0],
            out_shape=jax.ShapeDtypeStruct((slabs, WINDOW, LANES), jnp.bfloat16),
            scratch_shapes=[
                pltpu.VMEM((depth // LANES, LANES, LANES), jnp.bfloat16),
                pltpu.VMEM((1, STEP), jnp.float32),
                pltpu.VMEM((EDGE, LANES), jnp.float32),
                pltpu.SemaphoreType.DMA((depth // LANES + 1,)),
            ],
            compiler_params=pltpu.CompilerParams(vmem_limit_bytes=4 << 20),
            name="window_rows",
        )(in_hbm(own_data), in_hbm(depth_gain.reshape(1, STEP)))
        own = lax.all_to_all(windows, "slab", split_axis=0, concat_axis=0, tiled=True)
        places = [slab + step & slabs - 1 for step in (-1, 0, 1)]
    else:
        turned = jnp.pad(own_data.T, ((EDGE, EDGE), (0, 0)))
        windows = jnp.stack([turned[i * STEP : i * STEP + WINDOW] for i in range(slabs)])
        own = lax.all_to_all(windows, "slab", split_axis=0, concat_axis=0, tiled=True)
        own = own.transpose(1, 0, 2).reshape(WINDOW, elements // LANES, LANES).transpose(1, 0, 2)
        ring = [(i, (i + 1) % slabs) for i in range(slabs)]
        left = lax.ppermute(depth_gain, "slab", ring)
        right = lax.ppermute(depth_gain, "slab", [(j, i) for i, j in ring])
        high = lambda value: lax.reduce_precision(value, 8, 7)
        for place, value in enumerate((left, depth_gain, right)):
            middle = high(value - high(value))
            note = jnp.stack([high(value), middle, value - high(value) - middle])
            own = own.at[place, :3, :STEP].set(note.astype(jnp.bfloat16))
        places = [0, 1, 2]

    places = [jnp.asarray(place, jnp.int32) for place in places]
    gain_table = column_gain.reshape(-1, LANES)
    turn = (0, 1, 2, 4, 3)
    shifts = coarse_shift.transpose(turn)
    own_shapes = [(SPREAD, LANES), (LX * LY, LANES), (LX * LY, LANES)]
    own_shapes += [(2, GROUPS * 8, LANES), (GROUPS * SUMS, LANES)]
    kernel_arrays = pl.pallas_call(
        own_kernels,
        in_specs=[scalars] + on_chip(1) + [pl.BlockSpec(memory_space=pltpu.HBM)] * 3,
        out_specs=on_chip(9),
        out_shape=[pltpu.VMEM(shape, jnp.float32) for shape in own_shapes]
        + [
            pltpu.VMEM((8, LANES), jnp.int32),
            pltpu.VMEM(shifts.shape, jnp.int32),
            pltpu.VMEM((LANES, LX * LY // LANES), jnp.float32),
            pltpu.VMEM(migration.shape, jnp.bfloat16),
        ],
        scratch_shapes=[
            pltpu.VMEM((2 * BX * PACKED, LANES), jnp.float32),
            pltpu.VMEM((LX * LY // LANES, LANES), jnp.float32),
            pltpu.SemaphoreType.DMA((LX // LOAD + 2,)),
        ],
        compiler_params=pltpu.CompilerParams(vmem_limit_bytes=16 << 20),
        name="own_kernels",
    )(jnp.stack(places), pinned(own), in_hbm(migration), in_hbm(gain_table), in_hbm(shifts))

    kept = own
    received = own
    bit = 1
    while bit < frames:
        if bit > 1:
            mine = (chosen ^ frame) & (bit // 2) == 0
            kept = jnp.where(mine, kept, received)
        received = lax.ppermute(kept, "frame", [(i, i ^ bit) for i in range(frames)])
        bit *= 2
    keep = ((chosen ^ frame) & (frames // 2) == 0).astype(jnp.int32)
    choice = jnp.stack([keep] + places)

    shapes = [jax.ShapeDtypeStruct((n,) + shifts.shape[1:], jnp.float32) for n in (7, 3)]
    scores, displacement = pl.pallas_call(
        track,
        in_specs=[scalars] + on_chip(11),
        out_specs=on_chip(2),
        out_shape=shapes,
        scratch_shapes=[
            pltpu.VMEM((VOLUME, LANES), jnp.float32),
            pltpu.VMEM((12, GROUPS * SUMS, LANES), jnp.float32),
            pltpu.VMEM((LANES + 16, LANES), jnp.float32),
            pltpu.SMEM((8, LANES), jnp.int32),
            pltpu.SemaphoreType.DMA,
        ],
        compiler_params=pltpu.CompilerParams(vmem_limit_bytes=24 << 20),
        name="track",
    )(
        choice,
        pinned(kept),
        pinned(received),
        *[pinned(array) for array in kernel_arrays],
    )
    return scores.transpose(turn), displacement.transpose(turn)


def solution(mesh):
    blocks = P(None, "frame", None, None, "slab")
    placed = (P("slab", "frame", None), P(), P(), P("slab"), blocks, P())
    return jax.shard_map(
        per_device, mesh=mesh, in_specs=placed, out_specs=(blocks, blocks), check_vma=False
    )
```
